512 devices in a mesh: gx: 32 (over x, z), gy: 4 (over y_hi, core), dp: 4 (over y_lo).
Axes of the slice: x: 4, y: 8 (y_hi: 2, y_lo: 4; y = y_hi * 4 + y_lo), z: 8, core: 2. Of those that a mesh axis runs over, the one named last changes fastest.
Arguments:
- features: bfloat16 [4, 512, 1024, 128], P('dp', 'gx', 'gy'), may hold values from -6 to 6
- kernel: bfloat16 [3, 3, 3, 64, 64], replicated, may hold values from -0.15625 to 0.15625
- offsets: float32 [64], replicated, may hold values from -3 to 3
- upstream: bfloat16 [4, 512, 1024, 128], P('dp', 'gx', 'gy'), may hold values from -6 to 6
- grad_exponents: int32 [3, 3, 3], replicated, may hold values from -2 to 2
Outputs:
- activation: bfloat16 [4, 512, 1024, 128], P('dp', 'gx', 'gy')
- input_grad: bfloat16 [4, 512, 1024, 128], P('dp', 'gx', 'gy')
- kernel_grad: bfloat16 [3, 3, 3, 64, 64], P(None, None, None, None, 'dp')
- bias_grad: float32 [64], P('dp')
The draws below stay inside these ranges and needn't reach their ends.
All inputs are finite; a program needn't handle non-finite values.
Results may differ from the reference program's by a relative error of at most 0.007.
Values may be sent and summed in bfloat16 or wider, within the bound.
A program may use at most 128 MiB of HBM per device.

```python
import jax
import jax.numpy as jnp
from jax import lax

C = 64
PLANES = 2
SAMPLES = 4
NX = 512
NY = 1024


def with_ends(array, key, low, high):
    longest = array.shape.index(max(array.shape))
    spots = []
    for shift in (0, 1):
        where = [jax.random.randint(jax.random.fold_in(key, axis), (), 0, length) for axis, length in enumerate(array.shape)]
        where[longest] = (where[longest] + shift) % array.shape[longest]
        spots.append(tuple(where))
    return array.at[spots[0]].set(low).at[spots[1]].set(high)


def shard_levels(stream_key, dims, shards, low, largest):
    loudness, own = 1.0, jax.random.fold_in(stream_key, 6)
    for position, blocks in shards:
        steps = jnp.exp(jax.random.uniform(jax.random.fold_in(own, position), (blocks,), jnp.float32, low / len(shards), largest / len(shards)))
        loudness = loudness * jnp.repeat(steps, dims[position] // blocks).reshape([-1 if axis == position else 1 for axis in range(len(dims))])
    return loudness


def scatter_about(rng, shape, spread, bound, shards=(), dtype=jnp.bfloat16):
    array = spread * jax.random.normal(rng, shape, jnp.float32)
    if shards:
        array = array * shard_levels(rng, shape, shards, -0.22, 0.18)
    return jnp.clip(array, -bound, bound).astype(dtype)


def setup_inputs(seed: int = 0) -> dict:
    key_list = jax.random.split(jax.random.key(seed), 6)
    features = scatter_about(key_list[0], (SAMPLES, NX, NY, PLANES * C), 1.0, 6.0, ((0, 4), (1, 32), (2, 4)))
    kernel = scatter_about(key_list[1], (3, 3, 3, C, C), (27 * C) ** -0.5, 0.15625)
    offsets = scatter_about(key_list[2], (C,), 0.5, 3.0, (), jnp.float32)
    upstream = scatter_about(key_list[3], (SAMPLES, NX, NY, PLANES * C), 1.0, 6.0, ((0, 4), (1, 32), (2, 4)))
    grad_exponents = with_ends(jax.random.randint(key_list[4], (3, 3, 3), -2, 3), jax.random.fold_in(key_list[4], 1), -2, 2).astype(jnp.int32)
    return dict(features=features, kernel=kernel, offsets=offsets, upstream=upstream, grad_exponents=grad_exponents)


def build_matrices(kernel):
    upper = jnp.concatenate([kernel[:, :, 1], kernel[:, :, 0]], axis=-1)
    lower = jnp.concatenate([kernel[:, :, 2], kernel[:, :, 1]], axis=-1)
    return jnp.concatenate([upper, lower], axis=2)

def reference(features, kernel, offsets, upstream, grad_exponents):
    matrices = build_matrices(kernel)
    width = features.shape[3]
    chans = width // 2
    bias_full = jnp.concatenate([offsets, offsets]).astype(jnp.float32)

    def one_sample(pair):
        sample, cotangent = pair
        size_x, size_y = (sample.shape[0], sample.shape[1])
        padded = jnp.pad(sample, ((1, 1), (1, 1), (0, 0)))
        preact = jnp.zeros((size_x * size_y, width), jnp.float32) + bias_full
        for shift_x in range(3):
            for shift_y in range(3):
                window = padded[shift_x:shift_x + size_x, shift_y:shift_y + size_y].reshape(-1, width)
                preact = preact + jnp.dot(window, matrices[shift_x, shift_y], preferred_element_type=jnp.float32)
        sigma = jax.nn.sigmoid(preact)
        activation = (preact * sigma).astype(jnp.bfloat16)
        pre_grad = (cotangent.reshape(-1, width).astype(jnp.float32) * sigma * (1.0 + preact * (1.0 - sigma))).astype(jnp.bfloat16)
        grad_pad = jnp.pad(pre_grad.reshape(size_x, size_y, width), ((1, 1), (1, 1), (0, 0)))
        input_grad = jnp.zeros((size_x * size_y, width), jnp.float32)
        blocks = []
        for shift_x in range(3):
            for shift_y in range(3):
                window = grad_pad[2 - shift_x:2 - shift_x + size_x, 2 - shift_y:2 - shift_y + size_y].reshape(-1, width)
                input_grad = input_grad + jnp.dot(window, matrices[shift_x, shift_y].T, preferred_element_type=jnp.float32)
                source = padded[shift_x:shift_x + size_x, shift_y:shift_y + size_y].reshape(-1, width)
                blocks.append(jnp.dot(source.T, pre_grad, preferred_element_type=jnp.float32))
        matrix_grad = jnp.stack(blocks).reshape(3, 3, width, width)
        bias_sum = lax.optimization_barrier(jnp.sum(pre_grad.astype(jnp.float32), axis=0))
        return (activation.reshape(size_x, size_y, width), input_grad.astype(jnp.bfloat16).reshape(size_x, size_y, width), matrix_grad, bias_sum)
    activation, input_grad, matrix_grads, bias_sums = lax.map(one_sample, (features, upstream))
    matrix_grad = lax.optimization_barrier(jnp.sum(matrix_grads, axis=0))
    bias_sum = lax.optimization_barrier(jnp.sum(bias_sums, axis=0))
    tap_low = matrix_grad[:, :, :chans, chans:]
    tap_mid = matrix_grad[:, :, :chans, :chans] + matrix_grad[:, :, chans:, chans:]
    tap_high = matrix_grad[:, :, chans:, :chans]
    tap_grad = jnp.stack([tap_low, tap_mid, tap_high], axis=2)
    count = features.shape[0] * features.shape[1] * features.shape[2] * 2
    inverse = 1.0 / jnp.sqrt(jnp.float32(count))
    scales = jnp.exp2(grad_exponents.astype(jnp.float32))[:, :, :, None, None]
    kernel_grad = (tap_grad * scales * inverse).astype(jnp.bfloat16)
    bias_grad = (bias_sum[:chans] + bias_sum[chans:]) * inverse
    return (activation, input_grad, kernel_grad, bias_grad)
```

```python
import functools
import math

import jax
import jax.numpy as jnp
from jax import lax
from jax.experimental import pallas as pl
from jax.experimental.pallas import tpu as pltpu
from jax.sharding import PartitionSpec as P

MESH = pl.DeviceIdType.MESH


def extended(cells, sides, width):
    for axis, dim in sides:
        count = lax.axis_size(axis)
        ends = count - 1
        head = lax.slice_in_dim(cells, 0, width, axis=dim)
        tail = lax.slice_in_dim(cells, cells.shape[dim] - width, cells.shape[dim], axis=dim)
        cells = jnp.concatenate(
            [
                lax.ppermute(tail, axis, [(i, (i + 1) % count) for i in range(ends)]),
                cells,
                lax.ppermute(head, axis, [((i + 1) % count, i) for i in range(ends)]),
            ],
            axis=dim,
        )
    return cells


def build_matrices(kernel):
    upper = jnp.concatenate([kernel[:, :, 1], kernel[:, :, 0]], axis=-1)
    lower = jnp.concatenate([kernel[:, :, 2], kernel[:, :, 1]], axis=-1)
    return jnp.concatenate([upper, lower], axis=2)


def forward_conv(padded, matrices, size_x, size_y, bias_full):
    total = bias_full
    for shift_x in range(3):
        for shift_y in range(3):
            window = padded[:, shift_x : shift_x + size_x, shift_y : shift_y + size_y]
            total = total + jnp.einsum(
                "sxyc,cd->sxyd",
                window,
                matrices[shift_x, shift_y],
                preferred_element_type=jnp.float32,
            )
    return total


def backward_conv(grad_pad, matrices, size_x, size_y):
    total = None
    for shift_x in range(3):
        for shift_y in range(3):
            window = grad_pad[
                :, 2 - shift_x : 2 - shift_x + size_x, 2 - shift_y : 2 - shift_y + size_y
            ]
            term = jnp.einsum(
                "sxyd,cd->sxyc",
                window,
                matrices[shift_x, shift_y],
                preferred_element_type=jnp.float32,
            )
            total = term if total is None else total + term
    return total


def weight_blocks(source_pad, pre_grad, start, size_x, size_y):
    blocks = []
    for shift_x in range(3):
        for shift_y in range(3):
            window = source_pad[
                :,
                start + shift_x : start + shift_x + size_x,
                start + shift_y : start + shift_y + size_y,
            ]
            blocks.append(
                jnp.einsum("sxyd,sxyc->dc", pre_grad, window, preferred_element_type=jnp.float32)
            )
    return jnp.stack(blocks)


NX, NZ, NH, NC, ND = 4, 8, 2, 2, 4
NYL = NH * ND
TILES = 32


def place():
    gx, gy, d = lax.axis_index("gx"), lax.axis_index("gy"), lax.axis_index("dp")
    return gx // NZ, gx % NZ, gy // NC, gy % NC, d


def device(x, z, h, c, d):
    return {"gx": x * NZ + z, "gy": h * NC + c, "dp": d}


def peers(x, z, h, c, d):
    y = h * ND + d
    out = []
    for j in range(1, NC * NX * NH):
        out.append(device((x + (j // 2) % NX) % NX, z, (h + j // (2 * NX)) % NH, (c + j % 2) % NC, d))
    for k in range(1, NYL):
        if k != ND:
            other = (y + k) % NYL
            out.append(device(x, z, other // ND, c, other % ND))
    for k in range(1, NZ):
        out.append(device(x, (z + k) % NZ, h, c, d))
    return out


def reduce_kernel(
    v_ref, out_ref, cbuf, xbuf, ybuf, zbuf, acc1, acc2, acc3,
    csem, xsem, ysem, zsem, gsem,
):
    x, z, h, c, d = place()
    y = h * ND + d

    barrier = pltpu.get_barrier_semaphore()
    others = peers(x, z, h, c, d)
    for peer in others:
        pl.semaphore_signal(barrier, inc=1, device_id=peer, device_id_type=MESH)
    pl.semaphore_wait(barrier, len(others))

    def send(src, dst, sems, k, peer):
        copy = pltpu.make_async_remote_copy(
            src_ref=src, dst_ref=dst, send_sem=sems.at[0, k], recv_sem=sems.at[1, k],
            device_id=peer, device_id_type=MESH,
        )
        copy.start()
        return copy

    first = send(v_ref.at[1 - c], cbuf, csem, 0, device(x, z, h, 1 - c, d))
    first.wait_recv()
    acc1[...] = v_ref[c] + cbuf[...]

    copies_x = [
        send(acc1.at[(x + k) % NX], xbuf.at[k - 1], xsem, k - 1, device((x + k) % NX, z, h, c, d))
        for k in range(1, NX)
    ]
    for copy in copies_x:
        copy.wait_recv()
    acc2[...] = acc1[x] + xbuf[0] + xbuf[1] + xbuf[2]

    copies_y = []
    for k in range(1, NYL):
        other = (y + k) % NYL
        copies_y.append(
            send(acc2.at[other], ybuf.at[k - 1], ysem, k - 1, device(x, z, other // ND, c, other % ND))
        )
    for copy in copies_y:
        copy.wait_recv()
    total = acc2[y]
    for k in range(NYL - 1):
        total = total + ybuf[k]
    acc3[...] = total
    zbuf[z] = total

    copies_z = [
        send(acc3, zbuf.at[z], zsem, k - 1, device(x, (z + k) % NZ, h, c, d)) for k in range(1, NZ)
    ]
    for k in range(1, NZ):
        source = (z + NZ - k) % NZ
        pltpu.make_async_remote_copy(
            src_ref=acc3, dst_ref=zbuf.at[source], send_sem=zsem.at[0, k - 1], recv_sem=zsem.at[1, k - 1],
            device_id=device(x, source, h, c, d), device_id_type=MESH,
        ).wait_recv()
    total = zbuf[0]
    for k in range(1, NZ):
        total = total + zbuf[k]
    out_ref[c, x, h] = total

    copies_g = []
    for j in range(1, NC * NX * NH):
        peer = device((x + (j // 2) % NX) % NX, z, (h + j // (2 * NX)) % NH, (c + j % 2) % NC, d)
        copies_g.append(send(out_ref.at[c, x, h], out_ref.at[c, x, h], gsem, j - 1, peer))
    for j in range(1, NC * NX * NH):
        px, ph, pc = (x + NX - (j // 2) % NX) % NX, (h + NH - j // (2 * NX)) % NH, (c + NC - j % 2) % NC
        pltpu.make_async_remote_copy(
            src_ref=out_ref.at[pc, px, ph], dst_ref=out_ref.at[pc, px, ph],
            send_sem=gsem.at[0, j - 1], recv_sem=gsem.at[1, j - 1],
            device_id=device(px, z, ph, pc, d), device_id_type=MESH,
        ).wait_recv()
    for copy in [first] + copies_x + copies_y + copies_z + copies_g:
        copy.wait_send()


def reduced(pieces):
    f32 = jnp.float32
    return pl.pallas_call(
        reduce_kernel,
        out_shape=jax.ShapeDtypeStruct((NC, NX, NH, 2, 8, 128), f32),
        in_specs=[pl.BlockSpec(memory_space=pltpu.VMEM)],
        out_specs=pl.BlockSpec(memory_space=pltpu.VMEM),
        scratch_shapes=[
            pltpu.VMEM((NX, NYL, 2, 8, 128), f32),
            pltpu.VMEM((NX - 1, NYL, 2, 8, 128), f32),
            pltpu.VMEM((NYL - 1, 2, 8, 128), f32),
            pltpu.VMEM((NZ, 2, 8, 128), f32),
            pltpu.VMEM((NX, NYL, 2, 8, 128), f32),
            pltpu.VMEM((NYL, 2, 8, 128), f32),
            pltpu.VMEM((2, 8, 128), f32),
            pltpu.SemaphoreType.DMA((2, 1)),
            pltpu.SemaphoreType.DMA((2, NX - 1)),
            pltpu.SemaphoreType.DMA((2, NYL - 1)),
            pltpu.SemaphoreType.DMA((2, NZ - 1)),
            pltpu.SemaphoreType.DMA((2, NC * NX * NH - 1)),
        ],
        compiler_params=pltpu.CompilerParams(collective_id=0, has_side_effects=True),
        cost_estimate=pl.CostEstimate(flops=1_000_000, bytes_accessed=40_000_000, transcendentals=0),
    )(pieces)


def local(features, kernel, offsets, upstream, grad_exponents):
    matrices = build_matrices(kernel)
    size_x, size_y, width = (features.shape[1], features.shape[2], features.shape[3])
    chans = width // 2
    bias_full = jnp.concatenate([offsets, offsets])
    padded = extended(features, (("gx", 1), ("gy", 2)), 1)
    preact = forward_conv(padded, matrices, size_x, size_y, bias_full)
    sigma = jax.nn.sigmoid(preact)
    activation = (preact * sigma).astype(jnp.bfloat16)
    pre_grad = (upstream.astype(jnp.float32) * sigma * (1.0 + preact * (1.0 - sigma))).astype(
        jnp.bfloat16
    )
    grad_pad = extended(pre_grad, (("gx", 1), ("gy", 2)), 1)
    blocks = weight_blocks(padded, pre_grad, 0, size_x, size_y)
    input_grad = backward_conv(grad_pad, matrices, size_x, size_y).astype(jnp.bfloat16)
    summed = jnp.sum(pre_grad.astype(jnp.float32), axis=(0, 1, 2))
    bias_sum = summed[:chans] + summed[chans:]

    mid = blocks[:, :chans, :chans] + blocks[:, chans:, chans:]
    both = jnp.concatenate([mid, blocks[:, :chans, chans:]], axis=-1)
    low = jnp.concatenate(
        [blocks[:, chans:, :chans], jnp.broadcast_to(bias_sum[None, :, None], (1, chans, chans))]
    )
    packed = jnp.concatenate([both, jnp.concatenate([low[0::2], low[1::2]], axis=-1)])
    pieces = packed.reshape(14, ND, 2, 8, 128).transpose(1, 0, 2, 3, 4).reshape(ND, 28, 8, 128)
    pieces = jnp.pad(pieces, ((0, 0), (0, TILES - 28), (0, 0), (0, 0)))
    pieces = pieces.reshape(ND, NC, NX, NH, 2, 8, 128).transpose(1, 2, 3, 0, 4, 5, 6)
    total = reduced(pieces.reshape(NC, NX, NYL, 2, 8, 128))
    total = total.reshape(TILES, 8, 128)[:28].reshape(14, 16, 128)
    own = total.shape[1]
    low = total[9:].reshape(5, own, 2, chans).transpose(0, 2, 1, 3).reshape(10, own, chans)
    taps = jnp.stack([low[:9], total[:9, :, :chans], total[:9, :, chans:]], axis=1)
    tap_grad = taps.reshape(3, 3, 3, own, chans).swapaxes(3, 4)
    bias_sum = low[9, :, 0]

    count = (
        features.shape[0]
        * lax.axis_size("dp")
        * size_x
        * lax.axis_size("gx")
        * size_y
        * lax.axis_size("gy")
        * 2
    )
    inverse = 1.0 / math.sqrt(count)
    scales = jnp.exp2(grad_exponents.astype(jnp.float32))[:, :, :, None, None]
    kernel_grad = (tap_grad * scales * inverse).astype(jnp.bfloat16)
    bias_grad = bias_sum * inverse
    return (activation, input_grad, kernel_grad, bias_grad)


def solution(mesh):
    placed = (P("dp", "gx", "gy", None), P(), P(), P("dp", "gx", "gy", None), P())
    return jax.shard_map(
        local,
        mesh=mesh,
        in_specs=placed,
        out_specs=(
            P("dp", "gx", "gy", None),
            P("dp", "gx", "gy", None),
            P(None, None, None, None, "dp"),
            P("dp"),
        ),
        check_vma=False,
    )
```

```python
import contextlib
import functools
import math

import jax
import jax.numpy as jnp
from jax import lax
from jax.experimental import pallas as pl
from jax.experimental.pallas import tpu as pltpu
from jax.sharding import PartitionSpec as P

MESH = pl.DeviceIdType.MESH
F32, BF16 = jnp.float32, jnp.bfloat16

NX, NZ, NH, NC, ND = 4, 8, 2, 2, 4
NYL = NH * ND
GX, GY = NX * NZ, NH * NC
TILES = 32
KEPT = TILES // (NC * NX)

SX, SY, W, CH, PAD = 16, 256, 128, 64, 16
PY = SY + 2 * PAD
PACK = 80


def place():
    gx, gy, d = lax.axis_index("gx"), lax.axis_index("gy"), lax.axis_index("dp")
    return gx // NZ, gx % NZ, gy // NC, gy % NC, d


def device(x, z, h, c, d):
    return {"gx": x * NZ + z, "gy": h * NC + c, "dp": d}


def gather_peer(x, z, h, c, d, j):
    return device((x + j // NC) % NX, z, h, (c + j) % NC, d)


def body(
    f_hbm, u_hbm, k_hbm, o_hbm, act, ig, gat,
    fx, ux, gx_ref, ft, mf, mb, acc, bacc, e32, ebf, rbuf, rcol, ucol, c32, gedge,
    v, cbuf, acc1, xbuf, acc2, ybuf, zbuf, kern, offs,
    lsem, hsem, csem, xsem, ysem, zsem, gsem,
):
    scopes = contextlib.ExitStack()

    def mark(name):
        scopes.close()
        scopes.enter_context(jax.named_scope(name))

    x, z, h, c, d = place()
    gx, gy = lax.axis_index("gx"), lax.axis_index("gy")
    y = h * ND + d

    def at(dx, dy):
        return {"gx": (gx + dx + GX) % GX, "gy": (gy + dy + GY) % GY, "dp": d}

    def remote(src, dst, sems, s, r, peer):
        return pltpu.make_async_remote_copy(
            src_ref=src, dst_ref=dst, send_sem=sems.at[0, s], recv_sem=sems.at[1, r],
            device_id=peer, device_id_type=MESH,
        )

    mark("setup")
    load_f = pltpu.make_async_copy(f_hbm, fx.at[2 : 2 + SX, PAD : PAD + SY], lsem.at[0])
    load_u = pltpu.make_async_copy(u_hbm, ux.at[1 : 1 + SX, PAD : PAD + SY], lsem.at[1])
    load_k = pltpu.make_async_copy(k_hbm, kern, lsem.at[2])
    load_o = pltpu.make_async_copy(o_hbm, offs, lsem.at[3])
    load_k.start()
    load_o.start()
    load_f.start()
    load_u.start()

    top, bottom, left, right = gx > 0, gx < GX - 1, gy > 0, gy < GY - 1

    def blank(ref, *where):
        ref[where] = jnp.zeros(ref[where].shape, ref.dtype)

    @pl.when(jnp.logical_not(top))
    def _():
        blank(fx, slice(0, 2), slice(PAD, PAD + SY))
        blank(ux, slice(0, 1), slice(PAD, PAD + SY))

    @pl.when(jnp.logical_not(bottom))
    def _():
        blank(fx, slice(SX + 2, SX + 4), slice(PAD, PAD + SY))
        blank(ux, slice(SX + 1, SX + 2), slice(PAD, PAD + SY))

    for side, there in ((0, left), (1, right)):
        for rows, other in ((slice(0, 48), True), (slice(48, 64), top), (slice(64, 80), bottom)):
            @pl.when(jnp.logical_not(jnp.logical_and(there, other)))
            def _(side=side, rows=rows):
                blank(rbuf, side, rows)

    barrier = pltpu.get_barrier_semaphore()
    around = [at(dx, dy) for dx in (-1, 0, 1) for dy in (-1, 0, 1) if dx or dy]
    others = [gather_peer(x, z, h, c, d, j) for j in range(1, NC * NX)]
    for k in range(1, NYL):
        other = (y + k) % NYL
        others.append(device(x, z, other // ND, c, other % ND))
    for k in range(1, NZ):
        others.append(device(x, (z + k) % NZ, h, c, d))
    for peer in around + others:
        pl.semaphore_signal(barrier, inc=1, device_id=peer, device_id_type=MESH)

    load_k.wait()
    load_o.wait()
    for a in range(3):
        for b in range(3):
            k0, k1, k2 = kern[a, b, 0], kern[a, b, 1], kern[a, b, 2]
            m = jnp.concatenate(
                [jnp.concatenate([k1, k0], axis=1), jnp.concatenate([k2, k1], axis=1)], axis=0
            )
            mf[a * W : (a + 1) * W, b * W : (b + 1) * W] = m
            mb[(2 - b) * W : (3 - b) * W, (2 - a) * W : (3 - a) * W] = m
    bias = jnp.concatenate([offs[...], offs[...]], axis=1)
    c32[...] = jnp.zeros_like(c32)
    e32[...] = jnp.zeros_like(e32)
    acc[...] = jnp.zeros_like(acc)
    bacc[...] = jnp.zeros_like(bacc)

    mark("rims")
    load_f.wait()
    load_u.wait()

    for r in range(SX):
        for side, base in ((0, PAD), (1, PAD + SY - 16)):
            near, second = (0, 1) if side == 0 else (15, 14)
            tf = fx[2 + r, base : base + 16].astype(F32)
            tu = ux[1 + r, base : base + 16].astype(F32)
            nf, sf, nu = tf[near : near + 1], tf[second : second + 1], tu[near : near + 1]
            e32[side, r : r + 1] = nf
            e32[side, 16 + r : 17 + r] = sf
            e32[side, 32 + r : 33 + r] = nu
            for corner, first, edge in ((48, 0, 0), (64, SX - 2, SX - 1)):
                if first <= r < first + 2:
                    k = corner + r - first
                    e32[side, k : k + 1] = nf
                    e32[side, k + 2 : k + 3] = sf
                if r == edge:
                    e32[side, corner + 4 : corner + 5] = nu
    ebf[...] = e32[...].astype(BF16)

    mark("barrier")
    pl.semaphore_wait(barrier, len(around) + len(others))

    mark("send_rims")
    rows_y = slice(PAD, PAD + SY)
    halos = [
        (top, -1, 0, f_hbm.at[0:2], fx.at[SX + 2 : SX + 4, rows_y], 0, 1),
        (top, -1, 0, u_hbm.at[0:1], ux.at[SX + 1 : SX + 2, rows_y], 2, 3),
        (bottom, 1, 0, f_hbm.at[SX - 2 : SX], fx.at[0:2, rows_y], 1, 0),
        (bottom, 1, 0, u_hbm.at[SX - 1 : SX], ux.at[0:1, rows_y], 3, 2),
        (left, 0, -1, ebf.at[0, 0:48], rbuf.at[1, 0:48], 4, 5),
        (right, 0, 1, ebf.at[1, 0:48], rbuf.at[0, 0:48], 5, 4),
        (jnp.logical_and(left, top), -1, -1, ebf.at[0, 48:64], rbuf.at[1, 64:80], 6, 9),
        (jnp.logical_and(left, bottom), 1, -1, ebf.at[0, 64:80], rbuf.at[1, 48:64], 7, 8),
        (jnp.logical_and(right, top), -1, 1, ebf.at[1, 48:64], rbuf.at[0, 64:80], 8, 7),
        (jnp.logical_and(right, bottom), 1, 1, ebf.at[1, 64:80], rbuf.at[0, 48:64], 9, 6),
    ]
    for there, dx, dy, src, dst, s, r in halos:
        @pl.when(there)
        def _(dx=dx, dy=dy, src=src, dst=dst, s=s, r=r):
            remote(src, dst, hsem, s, r, at(dx, dy)).start()

    mark("transpose")
    @pl.loop(2, SX + 2)
    def _(r):
        ft[r] = fx[r, PAD : PAD + SY].T

    arrivals = [
        (top, fx.at[0:2, rows_y], 0), (bottom, fx.at[SX + 2 : SX + 4, rows_y], 1),
        (top, ux.at[0:1, rows_y], 2), (bottom, ux.at[SX + 1 : SX + 2, rows_y], 3),
        (left, rbuf.at[0, 0:48], 4), (right, rbuf.at[1, 0:48], 5),
        (jnp.logical_and(left, top), rbuf.at[0, 48:64], 6),
        (jnp.logical_and(left, bottom), rbuf.at[0, 64:80], 7),
        (jnp.logical_and(right, top), rbuf.at[1, 48:64], 8),
        (jnp.logical_and(right, bottom), rbuf.at[1, 64:80], 9),
    ]
    mark("await_rims")
    for there, dst, s in arrivals:
        @pl.when(there)
        def _(dst=dst, s=s):
            remote(dst, dst, hsem, s, s, at(0, 1)).wait_recv()

    mark("place_rims")
    ft[1] = fx[1, PAD : PAD + SY].T
    ft[SX + 2] = fx[SX + 2, PAD : PAD + SY].T

    for side in range(2):
        got = rbuf[side].astype(F32)
        rcol[side, 0, 2 : SX + 2] = got[0:16]
        rcol[side, 1, 2 : SX + 2] = got[16:32]
        for k in range(2):
            for n, row in ((k, 48), (SX + 2 + k, 64)):
                rcol[side, 0, n : n + 1] = got[row + k : row + k + 1]
                rcol[side, 1, n : n + 1] = got[row + 2 + k : row + 3 + k]
        ucol[side, 1 : SX + 1] = got[32:48]
        ucol[side, 0:1] = got[52:53]
        ucol[side, SX + 1 : SX + 2] = got[68:69]
        near, second = (15, 14) if side == 0 else (0, 1)
        base = 0 if side == 0 else PAD + SY
        for r in range(SX + 4):
            c32[r, near : near + 1] = rcol[side, 0, r : r + 1]
            c32[r, second : second + 1] = rcol[side, 1, r : r + 1]
        fx[:, base : base + PAD] = c32[...].astype(BF16)
        c32[:, second : second + 1] = jnp.zeros((SX + 4, 1, W), F32)
        for r in range(SX + 2):
            c32[r, near : near + 1] = ucol[side, r : r + 1]
        ux[:, base : base + PAD] = c32[0 : SX + 2].astype(BF16)
        c32[:, near : near + 1] = jnp.zeros((SX + 4, 1, W), F32)

    mark("forward")
    spot = lax.broadcasted_iota(jnp.int32, (SY, W), 0)

    @pl.loop(0, SX + 2)
    def _(r):
        window = jnp.concatenate([fx[r], fx[r + 1], fx[r + 2]], axis=1)
        p = jnp.dot(window, mf[...], preferred_element_type=F32)
        pre = (
            pltpu.roll(p[:, :W], 1, 0) + p[:, W : 2 * W] + pltpu.roll(p[:, 2 * W :], PY - 1, 0) + bias
        )
        sigma = jax.nn.sigmoid(pre)
        grad = (ux[r].astype(F32) * sigma * (1.0 + pre * (1.0 - sigma))).astype(BF16)
        gx_ref[r] = grad

        @pl.when(jnp.logical_and(r >= 1, r <= SX))
        def _():
            act[r - 1] = (pre * sigma)[PAD : PAD + SY].astype(BF16)
            g32 = grad.astype(F32)
            inner = g32[PAD : PAD + SY]
            bacc[...] += inner.reshape(SY // 8, 8, W).sum(axis=0)
            gedge[0, pl.ds(r - 1, 1)] = inner[0:1]
            gedge[1, pl.ds(r - 1, 1)] = inner[SY - 1 : SY]
            after = pltpu.roll(g32, PY - 1, 0)[PAD : PAD + SY]
            before = pltpu.roll(g32, 1, 0)[PAD : PAD + SY]
            after = jnp.where(spot == SY - 1, 0.0, after).astype(BF16)
            before = jnp.where(spot == 0, 0.0, before).astype(BF16)
            rhs = jnp.concatenate([after, grad[PAD : PAD + SY], before], axis=1)
            lhs = jnp.concatenate([ft[r], ft[r + 1], ft[r + 2]], axis=0)
            acc[...] += jnp.dot(lhs, rhs, preferred_element_type=F32)

    mark("rim_columns")

    for side in range(2):
        lhs = jnp.concatenate([rcol[side, 0, a + 1 : a + 1 + SX] for a in range(3)], axis=1)
        part = lax.dot_general(
            lhs.astype(BF16), gedge[side].astype(BF16), (((0,), (0,)), ((), ())), preferred_element_type=F32
        )
        acc[:, 2 * side * W : (2 * side + 1) * W] += part

    mark("pack")
    lane = lax.broadcasted_iota(jnp.int32, (CH, W), 1)

    def put(j, block):
        for dd in range(ND):
            for half in range(2):
                t = 2 * j + half
                v[t // (NX * KEPT), (t // KEPT) % NX, dd, t % KEPT] = block[
                    16 * dd + 8 * half : 16 * dd + 8 * half + 8
                ]

    lows = []
    for a in range(3):
        for b in range(3):
            t = acc[a * W : (a + 1) * W, b * W : (b + 1) * W].T
            turned = pltpu.roll(t[CH:], CH, 1)
            put(3 * a + b, t[:CH] + jnp.where(lane < CH, turned, 0.0))
            lows.append((t[CH:], turned))
    total = jnp.sum(bacc[...], axis=0, keepdims=True)
    col = jnp.broadcast_to(total, (W, W)).T
    lows.append((None, col[:CH] + col[CH:]))
    for k in range(5):
        put(9 + k, jnp.where(lane < CH, lows[2 * k][0], lows[2 * k + 1][1]))
    for t in range(28, TILES):
        for dd in range(ND):
            v[t // (NX * KEPT), (t // KEPT) % NX, dd, t % KEPT] = jnp.zeros((8, W), F32)

    def input_rows(first, last):
        @pl.loop(first, last)
        def _(r):
            window = jnp.concatenate([gx_ref[r], gx_ref[r + 1], gx_ref[r + 2]], axis=1)
            p = lax.dot_general(
                window, mb[...], (((1,), (1,)), ((), ())), preferred_element_type=F32
            )
            out = pltpu.roll(p[:, :W], 1, 0) + p[:, W : 2 * W] + pltpu.roll(p[:, 2 * W :], PY - 1, 0)
            ig[r] = out[PAD : PAD + SY].astype(BF16)

    sent = []
    mark("sum_cores")
    first = remote(v.at[1 - c], cbuf, csem, 0, 0, device(x, z, h, 1 - c, d))
    first.start()
    sent.append(first)
    first.wait_recv()
    acc1[...] = v[c] + cbuf[...]

    mark("sum_x")
    along = []
    for k in range(1, NX):
        other = (x + k) % NX
        copy = remote(acc1.at[other], xbuf.at[k - 1], xsem, k - 1, k - 1, device(other, z, h, c, d))
        copy.start()
        along.append(copy)
    sent += along
    input_rows(0, 6)
    for copy in along:
        copy.wait_recv()
    acc2[...] = acc1[x] + xbuf[0] + xbuf[1] + xbuf[2]

    mark("sum_y")
    ybuf[y] = acc2[d]
    for k in range(1, NYL):
        other = (y + k) % NYL
        copy = remote(
            acc2.at[other % ND], ybuf.at[y], ysem, k - 1, k - 1, device(x, z, other // ND, c, other % ND)
        )
        copy.start()
        sent.append(copy)
    input_rows(6, 11)
    for k in range(1, NYL):
        other = (y + NYL - k) % NYL
        slot = ybuf.at[other]
        remote(slot, slot, ysem, k - 1, k - 1, device(x, z, other // ND, c, other % ND)).wait_recv()
    part = ybuf[0]
    for k in range(1, NYL):
        part = part + ybuf[k]
    zbuf[z] = part

    mark("sum_z")
    for k in range(1, NZ):
        copy = remote(zbuf.at[z], zbuf.at[z], zsem, k - 1, k - 1, device(x, (z + k) % NZ, h, c, d))
        copy.start()
        sent.append(copy)
    input_rows(11, SX)
    for k in range(1, NZ):
        other = (z + NZ - k) % NZ
        slot = zbuf.at[other]
        remote(slot, slot, zsem, k - 1, k - 1, device(x, other, h, c, d)).wait_recv()
    part = zbuf[0]
    for k in range(1, NZ):
        part = part + zbuf[k]
    gat[c, x] = part

    mark("gather")
    for j in range(1, NC * NX):
        copy = remote(gat.at[c, x], gat.at[c, x], gsem, j - 1, j - 1, gather_peer(x, z, h, c, d, j))
        copy.start()
        sent.append(copy)
    for j in range(1, NC * NX):
        px, pc = (x + NX - j // NC) % NX, (c + NC - j % NC) % NC
        slot = gat.at[pc, px]
        remote(slot, slot, gsem, j - 1, j - 1, device(px, z, h, pc, d)).wait_recv()

    mark("drain")
    for copy in sent:
        copy.wait_send()
    for there, dx, dy, src, dst, s, r in halos:
        @pl.when(there)
        def _(dx=dx, dy=dy, src=src, dst=dst, s=s, r=r):
            remote(src, dst, hsem, s, r, at(dx, dy)).wait_send()
    scopes.close()


def finish(scale, act_in, ig_in, gat, exps, act_hbm, ig_hbm, kg_ref, bg_ref, lsem):
    copies = [
        pltpu.make_async_copy(act_in, act_hbm, lsem.at[0]),
        pltpu.make_async_copy(ig_in, ig_hbm, lsem.at[1]),
    ]
    for copy in copies:
        copy.start()

    def tile(j):
        t = 2 * j
        return jnp.concatenate(
            [gat[t // (NX * KEPT), (t // KEPT) % NX, t % KEPT + i] for i in range(2)], axis=0
        )

    def scaled(value, a, b, k):
        factor = jnp.exp2(jnp.full((16, CH), exps[a, b, k], jnp.int32).astype(F32)) * scale
        kg_ref[a, b, k] = (value * factor).astype(BF16)

    for j in range(9):
        both = tile(j)
        pair = tile(9 + j // 2)
        low = pair if j % 2 == 0 else pltpu.roll(pair, CH, 1)
        scaled(low[:, :CH], j // 3, j % 3, 0)
        scaled(both[:, :CH], j // 3, j % 3, 1)
        scaled(pltpu.roll(both, CH, 1)[:, :CH], j // 3, j % 3, 2)
    column = pltpu.roll(tile(13), CH, 1)[:, :16]
    same = lax.broadcasted_iota(jnp.int32, (16, 16), 0) == lax.broadcasted_iota(jnp.int32, (16, 16), 1)
    bg_ref[...] = jnp.sum(jnp.where(same, column, 0.0), axis=0, keepdims=True) * scale
    for copy in copies:
        copy.wait()


def local(features, kernel, offsets, upstream, grad_exponents):
    count = 4 * GX * GY * SX * SY * 2
    vmem, anywhere = pltpu.VMEM, pl.BlockSpec(memory_space=pl.ANY)
    hbm = pl.BlockSpec(memory_space=pltpu.HBM)
    in_vmem = pl.BlockSpec(memory_space=pltpu.VMEM)
    dma = pltpu.SemaphoreType.DMA
    activation, input_grad, gathered = pl.pallas_call(
        body,
        out_shape=(
            jax.ShapeDtypeStruct((SX, SY, W), BF16),
            jax.ShapeDtypeStruct((SX, SY, W), BF16),
            jax.ShapeDtypeStruct((NC, NX, KEPT, 8, W), F32),
        ),
        in_specs=[hbm, hbm, hbm, hbm],
        out_specs=(in_vmem, in_vmem, in_vmem),
        scratch_shapes=[
            vmem((SX + 4, PY, W), BF16),
            vmem((SX + 2, PY, W), BF16),
            vmem((SX + 2, PY, W), BF16),
            vmem((SX + 4, W, SY), BF16),
            vmem((3 * W, 3 * W), BF16),
            vmem((3 * W, 3 * W), BF16),
            vmem((3 * W, 3 * W), F32),
            vmem((8, W), F32),
            vmem((2, PACK, W), F32),
            vmem((2, PACK, W), BF16),
            vmem((2, PACK, W), BF16),
            vmem((2, 2, 24, W), F32),
            vmem((2, 24, W), F32),
            vmem((SX + 4, PAD, W), F32),
            vmem((2, SX, W), F32),
            vmem((NC, NX, ND, KEPT, 8, W), F32),
            vmem((NX, ND, KEPT, 8, W), F32),
            vmem((NX, ND, KEPT, 8, W), F32),
            vmem((NX - 1, ND, KEPT, 8, W), F32),
            vmem((ND, KEPT, 8, W), F32),
            vmem((NYL, KEPT, 8, W), F32),
            vmem((NZ, KEPT, 8, W), F32),
            vmem((3, 3, 3, CH, CH), BF16),
            vmem((1, CH), F32),
            dma((4,)),
            dma((2, 10)),
            dma((2, 1)),
            dma((2, NX - 1)),
            dma((2, NYL - 1)),
            dma((2, NZ - 1)),
            dma((2, NC * NX - 1)),
        ],
        compiler_params=pltpu.CompilerParams(
            collective_id=0, has_side_effects=True, vmem_limit_bytes=24 << 20
        ),
    )(
        pltpu.with_memory_space_constraint(features.reshape(SX, SY, W), pltpu.HBM),
        pltpu.with_memory_space_constraint(upstream.reshape(SX, SY, W), pltpu.HBM),
        pltpu.with_memory_space_constraint(kernel, pltpu.HBM),
        pltpu.with_memory_space_constraint(offsets.reshape(1, CH), pltpu.HBM),
    )
    activation, input_grad, kernel_grad, bias_grad = pl.pallas_call(
        functools.partial(finish, 1.0 / math.sqrt(count)),
        out_shape=(
            jax.ShapeDtypeStruct((SX, SY, W), BF16),
            jax.ShapeDtypeStruct((SX, SY, W), BF16),
            jax.ShapeDtypeStruct((3, 3, 3, 16, CH), BF16),
            jax.ShapeDtypeStruct((1, 16), F32),
        ),
        in_specs=[in_vmem, in_vmem, in_vmem, pl.BlockSpec(memory_space=pltpu.SMEM)],
        out_specs=(hbm, hbm, in_vmem, in_vmem),
        scratch_shapes=[dma((2,))],
        compiler_params=pltpu.CompilerParams(vmem_limit_bytes=24 << 20),
    )(activation, input_grad, gathered, grad_exponents)
    kernel_grad = kernel_grad.swapaxes(3, 4)
    return (
        activation.reshape(features.shape),
        input_grad.reshape(features.shape),
        kernel_grad,
        bias_grad.reshape(16),
    )


def solution(mesh):
    placed = (P("dp", "gx", "gy", None), P(), P(), P("dp", "gx", "gy", None), P())
    return jax.shard_map(
        local,
        mesh=mesh,
        in_specs=placed,
        out_specs=(
            P("dp", "gx", "gy", None),
            P("dp", "gx", "gy", None),
            P(None, None, None, None, "dp"),
            P("dp"),
        ),
        check_vma=False,
    )
```

```python
import contextlib
import functools
import math

import jax
import jax.numpy as jnp
from jax import lax
from jax.experimental import pallas as pl
from jax.experimental.pallas import tpu as pltpu
from jax.sharding import PartitionSpec as P

MESH = pl.DeviceIdType.MESH
F32, BF16 = jnp.float32, jnp.bfloat16

NX, NZ, NH, NC, ND = 4, 8, 2, 2, 4
NYL = NH * ND
GX, GY = NX * NZ, NH * NC

SX, SY, W, CH, PAD = 16, 256, 128, 64, 16
PY = SY + 2 * PAD
PACK = 80


def place():
    gx, gy, d = lax.axis_index("gx"), lax.axis_index("gy"), lax.axis_index("dp")
    return gx // NZ, gx % NZ, gy // NC, gy % NC, d


def device(x, z, h, c, d):
    return {"gx": x * NZ + z, "gy": h * NC + c, "dp": d}


def gather_peer(x, z, h, c, d, j):
    return device((x + j // NC) % NX, z, h, (c + j) % NC, d)


def body(
    f_hbm, u_hbm, k_hbm, o_hbm, act, ig, gat,
    fx, ux, gx_ref, ft, mf, mb, acc, bacc, e32, ebf, rbuf, rcol, ucol, gedge,
    v, cbuf, acc1, xbuf, acc2, ybuf, zbuf, kern, offs,
    lsem, hsem, csem, xsem, ysem, zsem, gsem,
):
    scopes = contextlib.ExitStack()

    def mark(name):
        scopes.close()
        scopes.enter_context(jax.named_scope(name))

    x, z, h, c, d = place()
    gx, gy = lax.axis_index("gx"), lax.axis_index("gy")
    y = h * ND + d

    def at(dx, dy):
        return {"gx": (gx + dx + GX) % GX, "gy": (gy + dy + GY) % GY, "dp": d}

    def remote(src, dst, sems, s, r, peer):
        return pltpu.make_async_remote_copy(
            src_ref=src, dst_ref=dst, send_sem=sems.at[0, s], recv_sem=sems.at[1, r],
            device_id=peer, device_id_type=MESH,
        )

    mark("setup")
    load_f = pltpu.make_async_copy(f_hbm, fx.at[2 : 2 + SX, PAD : PAD + SY], lsem.at[0])
    load_u = pltpu.make_async_copy(u_hbm, ux.at[1 : 1 + SX, PAD : PAD + SY], lsem.at[1])
    load_k = pltpu.make_async_copy(k_hbm, kern, lsem.at[2])
    load_o = pltpu.make_async_copy(o_hbm, offs, lsem.at[3])
    load_k.start()
    load_o.start()
    load_f.start()
    load_u.start()

    top, bottom, left, right = gx > 0, gx < GX - 1, gy > 0, gy < GY - 1

    barrier = pltpu.get_barrier_semaphore()
    around = [at(dx, dy) for dx in (-1, 0, 1) for dy in (-1, 0, 1) if dx or dy]
    others = [gather_peer(x, z, h, c, d, j) for j in range(1, NC * NX)]
    for k in range(1, NYL):
        other = (y + k) % NYL
        others.append(device(x, z, other // ND, c, other % ND))
    for k in range(1, NZ):
        others.append(device(x, (z + k) % NZ, h, c, d))
    for peer in around + others:
        pl.semaphore_signal(barrier, inc=1, device_id=peer, device_id_type=MESH)

    mark("barrier")
    pl.semaphore_wait(barrier, len(around) + len(others))

    mark("send_rims")
    rows_y = slice(PAD, PAD + SY)
    halos = [
        (top, -1, 0, f_hbm.at[0:2], fx.at[SX + 2 : SX + 4, rows_y], 0, 1),
        (top, -1, 0, u_hbm.at[0:1], ux.at[SX + 1 : SX + 2, rows_y], 2, 3),
        (bottom, 1, 0, f_hbm.at[SX - 2 : SX], fx.at[0:2, rows_y], 1, 0),
        (bottom, 1, 0, u_hbm.at[SX - 1 : SX], ux.at[0:1, rows_y], 3, 2),
        (left, 0, -1, ebf.at[0, 0:48], rbuf.at[1, 0:48], 4, 5),
        (right, 0, 1, ebf.at[1, 0:48], rbuf.at[0, 0:48], 5, 4),
        (jnp.logical_and(left, top), -1, -1, ebf.at[0, 48:64], rbuf.at[1, 64:80], 6, 9),
        (jnp.logical_and(left, bottom), 1, -1, ebf.at[0, 64:80], rbuf.at[1, 48:64], 7, 8),
        (jnp.logical_and(right, top), -1, 1, ebf.at[1, 48:64], rbuf.at[0, 64:80], 8, 7),
        (jnp.logical_and(right, bottom), 1, 1, ebf.at[1, 64:80], rbuf.at[0, 48:64], 9, 6),
    ]
    for there, dx, dy, src, dst, s, r in halos[:4]:
        @pl.when(there)
        def _(dx=dx, dy=dy, src=src, dst=dst, s=s, r=r):
            remote(src, dst, hsem, s, r, at(dx, dy)).start()

    mark("rims")
    load_f.wait()
    load_u.wait()
    e32[...] = jnp.zeros_like(e32)

    for r in range(SX):
        for side, base in ((0, PAD), (1, PAD + SY - 16)):
            near, second = (0, 1) if side == 0 else (15, 14)
            tf = fx[2 + r, base : base + 16].astype(F32)
            tu = ux[1 + r, base : base + 16].astype(F32)
            nf, sf, nu = tf[near : near + 1], tf[second : second + 1], tu[near : near + 1]
            e32[side, r : r + 1] = nf
            e32[side, 16 + r : 17 + r] = sf
            e32[side, 32 + r : 33 + r] = nu
            for corner, first, edge in ((48, 0, 0), (64, SX - 2, SX - 1)):
                if first <= r < first + 2:
                    k = corner + r - first
                    e32[side, k : k + 1] = nf
                    e32[side, k + 2 : k + 3] = sf
                if r == edge:
                    e32[side, corner + 4 : corner + 5] = nu
    ebf[...] = e32[...].astype(BF16)

    for there, dx, dy, src, dst, s, r in halos[4:]:
        @pl.when(there)
        def _(dx=dx, dy=dy, src=src, dst=dst, s=s, r=r):
            remote(src, dst, hsem, s, r, at(dx, dy)).start()

    mark("matrices")
    def blank(ref, *where):
        ref[where] = jnp.zeros(ref[where].shape, ref.dtype)

    @pl.when(jnp.logical_not(top))
    def _():
        blank(fx, slice(0, 2), slice(PAD, PAD + SY))
        blank(ux, slice(0, 1), slice(PAD, PAD + SY))

    @pl.when(jnp.logical_not(bottom))
    def _():
        blank(fx, slice(SX + 2, SX + 4), slice(PAD, PAD + SY))
        blank(ux, slice(SX + 1, SX + 2), slice(PAD, PAD + SY))

    for side, there in ((0, left), (1, right)):
        for rows, other in ((slice(0, 48), True), (slice(48, 64), top), (slice(64, 80), bottom)):
            @pl.when(jnp.logical_not(jnp.logical_and(there, other)))
            def _(side=side, rows=rows):
                blank(rbuf, side, rows)

    load_k.wait()
    load_o.wait()
    for a in range(3):
        for b in range(3):
            k0, k1, k2 = kern[a, b, 0], kern[a, b, 1], kern[a, b, 2]
            m = jnp.concatenate(
                [jnp.concatenate([k1, k0], axis=1), jnp.concatenate([k2, k1], axis=1)], axis=0
            )
            mf[a * W : (a + 1) * W, b * W : (b + 1) * W] = m
            mb[(2 - b) * W : (3 - b) * W, (2 - a) * W : (3 - a) * W] = m
    bias = jnp.concatenate([offs[...], offs[...]], axis=1)
    acc[...] = jnp.zeros_like(acc)
    bacc[...] = jnp.zeros_like(bacc)

    mark("transpose")
    @pl.loop(2, SX + 2)
    def _(r):
        ft[r] = fx[r, PAD : PAD + SY].T

    arrivals = [
        (top, fx.at[0:2, rows_y], 0), (bottom, fx.at[SX + 2 : SX + 4, rows_y], 1),
        (top, ux.at[0:1, rows_y], 2), (bottom, ux.at[SX + 1 : SX + 2, rows_y], 3),
        (left, rbuf.at[0, 0:48], 4), (right, rbuf.at[1, 0:48], 5),
        (jnp.logical_and(left, top), rbuf.at[0, 48:64], 6),
        (jnp.logical_and(left, bottom), rbuf.at[0, 64:80], 7),
        (jnp.logical_and(right, top), rbuf.at[1, 48:64], 8),
        (jnp.logical_and(right, bottom), rbuf.at[1, 64:80], 9),
    ]
    mark("await_rims")
    for there, dst, s in arrivals:
        @pl.when(there)
        def _(dst=dst, s=s):
            remote(dst, dst, hsem, s, s, at(0, 1)).wait_recv()

    mark("place_rims")
    ft[1] = fx[1, PAD : PAD + SY].T
    ft[SX + 2] = fx[SX + 2, PAD : PAD + SY].T

    for side in range(2):
        got = rbuf[side].astype(F32)
        rcol[side, 0, 2 : SX + 2] = got[0:16]
        rcol[side, 1, 2 : SX + 2] = got[16:32]
        for k in range(2):
            for n, row in ((k, 48), (SX + 2 + k, 64)):
                rcol[side, 0, n : n + 1] = got[row + k : row + k + 1]
                rcol[side, 1, n : n + 1] = got[row + 2 + k : row + 3 + k]
        ucol[side, 1 : SX + 1] = got[32:48]
        ucol[side, 0:1] = got[52:53]
        ucol[side, SX + 1 : SX + 2] = got[68:69]
        base = 0 if side == 0 else PAD + SY
        sub = lax.broadcasted_iota(jnp.int32, (8, W), 0)
        near, second = (7, 6) if side == 0 else (0, 1)
        empty = jnp.zeros((8, W), F32)

        def spread(rows):
            return jnp.broadcast_to(rows, (8, W))

        def padded(half):
            return jnp.concatenate([empty, half] if side == 0 else [half, empty], axis=0).astype(BF16)

        for r in range(SX + 4):
            other = jnp.where(sub == second, spread(rcol[side, 1, r : r + 1]), 0.0)
            half = jnp.where(sub == near, spread(rcol[side, 0, r : r + 1]), other)
            fx[r, base : base + PAD] = padded(half)
        for r in range(SX + 2):
            half = jnp.where(sub == near, spread(ucol[side, r : r + 1]), 0.0)
            ux[r, base : base + PAD] = padded(half)

    mark("forward")
    spot = lax.broadcasted_iota(jnp.int32, (SY, W), 0)

    def forward_row(r):
        window = jnp.concatenate([fx[r], fx[r + 1], fx[r + 2]], axis=1)
        p = jnp.dot(window, mf[...], preferred_element_type=F32)
        pre = (
            pltpu.roll(p[:, :W], 1, 0) + p[:, W : 2 * W] + pltpu.roll(p[:, 2 * W :], PY - 1, 0) + bias
        )
        sigma = jax.nn.sigmoid(pre)
        grad = (ux[r].astype(F32) * sigma * (1.0 + pre * (1.0 - sigma))).astype(BF16)
        gx_ref[r] = grad
        return pre, sigma, grad

    def weight_row(r):
        pre, sigma, grad = forward_row(r)
        act[r - 1] = (pre * sigma)[PAD : PAD + SY].astype(BF16)
        g32 = grad.astype(F32)
        inner = g32[PAD : PAD + SY]
        bacc[...] += inner.reshape(SY // 8, 8, W).sum(axis=0)
        gedge[0, pl.ds(r - 1, 1)] = inner[0:1]
        gedge[1, pl.ds(r - 1, 1)] = inner[SY - 1 : SY]
        after = pltpu.roll(g32, PY - 1, 0)[PAD : PAD + SY]
        before = pltpu.roll(g32, 1, 0)[PAD : PAD + SY]
        after = jnp.where(spot == SY - 1, 0.0, after).astype(BF16)
        before = jnp.where(spot == 0, 0.0, before).astype(BF16)
        return jnp.concatenate([after, grad[PAD : PAD + SY], before], axis=1)

    @pl.loop(0, SX // 16)
    def _(step):
        for k in range(0, 16, 4):
            r = step * 16 + k + 1
            rhs = jnp.concatenate([weight_row(r + n) for n in range(4)], axis=0)
            lhs = jnp.concatenate(
                [jnp.concatenate([ft[r + n + a] for n in range(4)], axis=1) for a in range(3)], axis=0
            )
            acc[...] += jnp.dot(lhs, rhs, preferred_element_type=F32)


    mark("rim_columns")

    for side in range(2):
        lhs = jnp.concatenate([rcol[side, 0, a + 1 : a + 1 + SX] for a in range(3)], axis=1)
        part = lax.dot_general(
            lhs.astype(BF16), gedge[side].astype(BF16), (((0,), (0,)), ((), ())), preferred_element_type=F32
        )
        acc[:, 2 * side * W : (2 * side + 1) * W] += part

    mark("pack")
    lane = lax.broadcasted_iota(jnp.int32, (CH, W), 1)

    def put(j, block):
        m = j // 2
        v[m // NX, m % NX, j % 2] = block

    highs = []
    for a in range(3):
        for b in range(3):
            t = acc[a * W : (a + 1) * W, b * W : (b + 1) * W]
            turned = pltpu.roll(t[CH:], CH, 1)
            put(3 * a + b, t[:CH] + jnp.where(lane < CH, turned, 0.0))
            highs.append((t[CH:], turned))
    total = jnp.sum(bacc[...], axis=0, keepdims=True)
    total = jnp.broadcast_to(total, (CH, W))
    highs.append((None, total + pltpu.roll(total, CH, 1)))
    for k in range(5):
        put(9 + k, jnp.where(lane < CH, highs[2 * k][0], highs[2 * k + 1][1]))
    for j in (14, 15):
        put(j, jnp.zeros((CH, W), F32))

    def input_rows(first, last):
        @pl.loop(first, last)
        def _(r):
            window = jnp.concatenate([gx_ref[r], gx_ref[r + 1], gx_ref[r + 2]], axis=1)
            p = lax.dot_general(
                window, mb[...], (((1,), (1,)), ((), ())), preferred_element_type=F32
            )
            out = pltpu.roll(p[:, :W], 1, 0) + p[:, W : 2 * W] + pltpu.roll(p[:, 2 * W :], PY - 1, 0)
            ig[r] = out[PAD : PAD + SY].astype(BF16)

    sent = []
    mark("sum_cores")
    first = remote(v.at[1 - c], cbuf, csem, 0, 0, device(x, z, h, 1 - c, d))
    first.start()
    sent.append(first)
    first.wait_recv()
    acc1[...] = v[c] + cbuf[...]

    mark("sum_x")
    along = []
    for k in range(1, NX):
        other = (x + k) % NX
        copy = remote(acc1.at[other], xbuf.at[k - 1], xsem, k - 1, k - 1, device(other, z, h, c, d))
        copy.start()
        along.append(copy)
    sent += along
    forward_row(0)
    forward_row(SX + 1)
    input_rows(0, 5)
    for copy in along:
        copy.wait_recv()
    pair = (acc1[x] + xbuf[0] + xbuf[1] + xbuf[2]).reshape(W, W).T
    for dd in range(ND):
        acc2[dd, 0] = pair[16 * dd : 16 * dd + 16]
        acc2[dd, 1] = pair[CH + 16 * dd : CH + 16 * dd + 16]

    mark("sum_y")
    ybuf[y] = acc2[d]
    for k in range(1, NYL):
        other = (y + k) % NYL
        copy = remote(
            acc2.at[other % ND], ybuf.at[y], ysem, k - 1, k - 1, device(x, z, other // ND, c, other % ND)
        )
        copy.start()
        sent.append(copy)
    input_rows(5, 11)
    for k in range(1, NYL):
        other = (y + NYL - k) % NYL
        slot = ybuf.at[other]
        remote(slot, slot, ysem, k - 1, k - 1, device(x, z, other // ND, c, other % ND)).wait_recv()
    part = ybuf[0]
    for k in range(1, NYL):
        part = part + ybuf[k]
    zbuf[z] = part

    mark("sum_z")
    for k in range(1, NZ):
        copy = remote(zbuf.at[z], zbuf.at[z], zsem, k - 1, k - 1, device(x, (z + k) % NZ, h, c, d))
        copy.start()
        sent.append(copy)
    input_rows(11, SX)
    for k in range(1, NZ):
        other = (z + NZ - k) % NZ
        slot = zbuf.at[other]
        remote(slot, slot, zsem, k - 1, k - 1, device(x, other, h, c, d)).wait_recv()
    part = zbuf[0]
    for k in range(1, NZ):
        part = part + zbuf[k]
    gat[c, x] = part

    mark("gather")
    for j in range(1, NC * NX):
        copy = remote(gat.at[c, x], gat.at[c, x], gsem, j - 1, j - 1, gather_peer(x, z, h, c, d, j))
        copy.start()
        sent.append(copy)
    for j in range(1, NC * NX):
        px, pc = (x + NX - j // NC) % NX, (c + NC - j % NC) % NC
        slot = gat.at[pc, px]
        remote(slot, slot, gsem, j - 1, j - 1, device(px, z, h, pc, d)).wait_recv()

    mark("drain")
    for copy in sent:
        copy.wait_send()
    for there, dx, dy, src, dst, s, r in halos:
        @pl.when(there)
        def _(dx=dx, dy=dy, src=src, dst=dst, s=s, r=r):
            remote(src, dst, hsem, s, r, at(dx, dy)).wait_send()
    scopes.close()


def finish(scale, act_in, ig_in, gat, exps, act_hbm, ig_hbm, kg_ref, bg_ref, lsem):
    copies = [
        pltpu.make_async_copy(act_in, act_hbm, lsem.at[0]),
        pltpu.make_async_copy(ig_in, ig_hbm, lsem.at[1]),
    ]
    for copy in copies:
        copy.start()

    def tile(j, half):
        m = j // 2
        block = gat[m // NX, m % NX, half]
        return block if j % 2 == 0 else pltpu.roll(block, CH, 1)

    def scaled(value, a, b, k):
        factor = jnp.exp2(jnp.full((16, CH), exps[a, b, k], jnp.int32).astype(F32)) * scale
        kg_ref[a, b, k] = (value * factor).astype(BF16)

    for j in range(9):
        scaled(tile(j, 1)[:, :CH], j // 3, j % 3, 0)
        scaled(tile(j, 0)[:, :CH], j // 3, j % 3, 1)
        scaled(tile(9 + j // 2, j % 2)[:, :CH], j // 3, j % 3, 2)
    column = tile(13, 1)[:, :16]
    same = lax.broadcasted_iota(jnp.int32, (16, 16), 0) == lax.broadcasted_iota(jnp.int32, (16, 16), 1)
    bg_ref[...] = jnp.sum(jnp.where(same, column, 0.0), axis=0, keepdims=True) * scale
    for copy in copies:
        copy.wait()


def local(features, kernel, offsets, upstream, grad_exponents):
    count = 4 * GX * GY * SX * SY * 2
    vmem, anywhere = pltpu.VMEM, pl.BlockSpec(memory_space=pl.ANY)
    hbm = pl.BlockSpec(memory_space=pltpu.HBM)
    in_vmem = pl.BlockSpec(memory_space=pltpu.VMEM)
    dma = pltpu.SemaphoreType.DMA
    activation, input_grad, gathered = pl.pallas_call(
        body,
        out_shape=(
            jax.ShapeDtypeStruct((SX, SY, W), BF16),
            jax.ShapeDtypeStruct((SX, SY, W), BF16),
            jax.ShapeDtypeStruct((NC, NX, 2, 16, W), F32),
        ),
        in_specs=[hbm, hbm, hbm, hbm],
        out_specs=(in_vmem, in_vmem, in_vmem),
        scratch_shapes=[
            vmem((SX + 4, PY, W), BF16),
            vmem((SX + 2, PY, W), BF16),
            vmem((SX + 2, PY, W), BF16),
            vmem((SX + 4, W, SY), BF16),
            vmem((3 * W, 3 * W), BF16),
            vmem((3 * W, 3 * W), BF16),
            vmem((3 * W, 3 * W), F32),
            vmem((8, W), F32),
            vmem((2, PACK, W), F32),
            vmem((2, PACK, W), BF16),
            vmem((2, PACK, W), BF16),
            vmem((2, 2, 24, W), F32),
            vmem((2, 24, W), F32),
            vmem((2, SX, W), F32),
            vmem((NC, NX, 2, CH, W), F32),
            vmem((NX, 2, CH, W), F32),
            vmem((NX, 2, CH, W), F32),
            vmem((NX - 1, 2, CH, W), F32),
            vmem((ND, 2, 16, W), F32),
            vmem((NYL, 2, 16, W), F32),
            vmem((NZ, 2, 16, W), F32),
            vmem((3, 3, 3, CH, CH), BF16),
            vmem((1, CH), F32),
            dma((4,)),
            dma((2, 10)),
            dma((2, 1)),
            dma((2, NX - 1)),
            dma((2, NYL - 1)),
            dma((2, NZ - 1)),
            dma((2, NC * NX - 1)),
        ],
        compiler_params=pltpu.CompilerParams(
            collective_id=0, has_side_effects=True, vmem_limit_bytes=24 << 20
        ),
    )(
        pltpu.with_memory_space_constraint(features.reshape(SX, SY, W), pltpu.HBM),
        pltpu.with_memory_space_constraint(upstream.reshape(SX, SY, W), pltpu.HBM),
        pltpu.with_memory_space_constraint(kernel, pltpu.HBM),
        pltpu.with_memory_space_constraint(offsets.reshape(1, CH), pltpu.HBM),
    )
    activation, input_grad, kernel_grad, bias_grad = pl.pallas_call(
        functools.partial(finish, 1.0 / math.sqrt(count)),
        out_shape=(
            jax.ShapeDtypeStruct((SX, SY, W), BF16),
            jax.ShapeDtypeStruct((SX, SY, W), BF16),
            jax.ShapeDtypeStruct((3, 3, 3, 16, CH), BF16),
            jax.ShapeDtypeStruct((1, 16), F32),
        ),
        in_specs=[in_vmem, in_vmem, in_vmem, pl.BlockSpec(memory_space=pltpu.SMEM)],
        out_specs=(hbm, hbm, in_vmem, in_vmem),
        scratch_shapes=[dma((2,))],
        compiler_params=pltpu.CompilerParams(vmem_limit_bytes=24 << 20),
    )(activation, input_grad, gathered, grad_exponents)
    kernel_grad = kernel_grad.swapaxes(3, 4)
    return (
        activation.reshape(features.shape),
        input_grad.reshape(features.shape),
        kernel_grad,
        bias_grad.reshape(16),
    )


def solution(mesh):
    placed = (P("dp", "gx", "gy", None), P(), P(), P("dp", "gx", "gy", None), P())
    return jax.shard_map(
        local,
        mesh=mesh,
        in_specs=placed,
        out_specs=(
            P("dp", "gx", "gy", None),
            P("dp", "gx", "gy", None),
            P(None, None, None, None, "dp"),
            P("dp"),
        ),
        check_vma=False,
    )
```

```python
import contextlib
import functools
import math

import jax
import jax.numpy as jnp
from jax import lax
from jax.experimental import pallas as pl
from jax.experimental.pallas import tpu as pltpu
from jax.sharding import PartitionSpec as P

MESH = pl.DeviceIdType.MESH
F32, BF16 = jnp.float32, jnp.bfloat16

NX, NZ, NH, NC, ND = 4, 8, 2, 2, 4
NYL = NH * ND
GX, GY = NX * NZ, NH * NC

SX, SY, W, CH, PAD = 16, 256, 128, 64, 16
PY = SY + 2 * PAD
PACK = 80


def place():
    gx, gy, d = lax.axis_index("gx"), lax.axis_index("gy"), lax.axis_index("dp")
    return gx // NZ, gx % NZ, gy // NC, gy % NC, d


def device(x, z, h, c, d):
    return {"gx": x * NZ + z, "gy": h * NC + c, "dp": d}


def gather_peer(x, z, h, c, d, j):
    return device((x + j // NC) % NX, z, h, (c + j) % NC, d)


def body(
    f_hbm, u_hbm, k_hbm, o_hbm, act, ig, gat,
    fx, ux, gx_ref, ft, mf, mb, acc, bacc, e32, ebf, rbuf, rcol, ucol, gedge,
    v, cbuf, acc1, acc1b, xbuf, acc2, ybuf, zbuf, kern, offs,
    lsem, hsem, csem, xsem, ysem, zsem, gsem,
):
    scopes = contextlib.ExitStack()

    def mark(name):
        scopes.close()
        scopes.enter_context(jax.named_scope(name))

    x, z, h, c, d = place()
    gx, gy = lax.axis_index("gx"), lax.axis_index("gy")
    y = h * ND + d

    def at(dx, dy):
        return {"gx": (gx + dx + GX) % GX, "gy": (gy + dy + GY) % GY, "dp": d}

    def remote(src, dst, sems, s, r, peer):
        return pltpu.make_async_remote_copy(
            src_ref=src, dst_ref=dst, send_sem=sems.at[0, s], recv_sem=sems.at[1, r],
            device_id=peer, device_id_type=MESH,
        )

    mark("setup")
    load_f = pltpu.make_async_copy(f_hbm, fx.at[2 : 2 + SX, PAD : PAD + SY], lsem.at[0])
    load_u = pltpu.make_async_copy(u_hbm, ux.at[1 : 1 + SX, PAD : PAD + SY], lsem.at[1])
    load_k = pltpu.make_async_copy(k_hbm, kern, lsem.at[2])
    load_o = pltpu.make_async_copy(o_hbm, offs, lsem.at[3])
    load_k.start()
    load_o.start()
    load_f.start()
    load_u.start()

    top, bottom, left, right = gx > 0, gx < GX - 1, gy > 0, gy < GY - 1

    barrier = pltpu.get_barrier_semaphore()
    around = [at(dx, dy) for dx in (-1, 0, 1) for dy in (-1, 0, 1) if dx or dy]
    others = [gather_peer(x, z, h, c, d, j) for j in range(1, NC * NX)]
    for k in range(1, NYL):
        other = (y + k) % NYL
        others.append(device(x, z, other // ND, c, other % ND))
    for k in range(1, NZ):
        others.append(device(x, (z + k) % NZ, h, c, d))
    for peer in around + others:
        pl.semaphore_signal(barrier, inc=1, device_id=peer, device_id_type=MESH)

    mark("barrier")
    pl.semaphore_wait(barrier, len(around) + len(others))

    mark("send_rims")
    rows_y = slice(PAD, PAD + SY)
    halos = [
        (top, -1, 0, f_hbm.at[0:2], fx.at[SX + 2 : SX + 4, rows_y], 0, 1),
        (top, -1, 0, u_hbm.at[0:1], ux.at[SX + 1 : SX + 2, rows_y], 2, 3),
        (bottom, 1, 0, f_hbm.at[SX - 2 : SX], fx.at[0:2, rows_y], 1, 0),
        (bottom, 1, 0, u_hbm.at[SX - 1 : SX], ux.at[0:1, rows_y], 3, 2),
        (left, 0, -1, ebf.at[0, 0:48], rbuf.at[1, 0:48], 4, 5),
        (right, 0, 1, ebf.at[1, 0:48], rbuf.at[0, 0:48], 5, 4),
        (jnp.logical_and(left, top), -1, -1, ebf.at[0, 48:64], rbuf.at[1, 64:80], 6, 9),
        (jnp.logical_and(left, bottom), 1, -1, ebf.at[0, 64:80], rbuf.at[1, 48:64], 7, 8),
        (jnp.logical_and(right, top), -1, 1, ebf.at[1, 48:64], rbuf.at[0, 64:80], 8, 7),
        (jnp.logical_and(right, bottom), 1, 1, ebf.at[1, 64:80], rbuf.at[0, 48:64], 9, 6),
    ]
    for there, dx, dy, src, dst, s, r in halos[:4]:
        @pl.when(there)
        def _(dx=dx, dy=dy, src=src, dst=dst, s=s, r=r):
            remote(src, dst, hsem, s, r, at(dx, dy)).start()

    mark("rims")
    load_f.wait()
    load_u.wait()
    e32[...] = jnp.zeros_like(e32)

    for r in range(SX):
        for side, base in ((0, PAD), (1, PAD + SY - 16)):
            near, second = (0, 1) if side == 0 else (15, 14)
            tf = fx[2 + r, base : base + 16].astype(F32)
            tu = ux[1 + r, base : base + 16].astype(F32)
            nf, sf, nu = tf[near : near + 1], tf[second : second + 1], tu[near : near + 1]
            e32[side, r : r + 1] = nf
            e32[side, 16 + r : 17 + r] = sf
            e32[side, 32 + r : 33 + r] = nu
            for corner, first, edge in ((48, 0, 0), (64, SX - 2, SX - 1)):
                if first <= r < first + 2:
                    k = corner + r - first
                    e32[side, k : k + 1] = nf
                    e32[side, k + 2 : k + 3] = sf
                if r == edge:
                    e32[side, corner + 4 : corner + 5] = nu
    ebf[...] = e32[...].astype(BF16)

    for there, dx, dy, src, dst, s, r in halos[4:]:
        @pl.when(there)
        def _(dx=dx, dy=dy, src=src, dst=dst, s=s, r=r):
            remote(src, dst, hsem, s, r, at(dx, dy)).start()

    mark("matrices")
    def blank(ref, *where):
        ref[where] = jnp.zeros(ref[where].shape, ref.dtype)

    @pl.when(jnp.logical_not(top))
    def _():
        blank(fx, slice(0, 2), slice(PAD, PAD + SY))
        blank(ux, slice(0, 1), slice(PAD, PAD + SY))

    @pl.when(jnp.logical_not(bottom))
    def _():
        blank(fx, slice(SX + 2, SX + 4), slice(PAD, PAD + SY))
        blank(ux, slice(SX + 1, SX + 2), slice(PAD, PAD + SY))

    for side, there in ((0, left), (1, right)):
        for rows, other in ((slice(0, 48), True), (slice(48, 64), top), (slice(64, 80), bottom)):
            @pl.when(jnp.logical_not(jnp.logical_and(there, other)))
            def _(side=side, rows=rows):
                blank(rbuf, side, rows)

    load_k.wait()
    load_o.wait()
    for a in range(3):
        for b in range(3):
            k0, k1, k2 = kern[a, b, 0], kern[a, b, 1], kern[a, b, 2]
            m = jnp.concatenate(
                [jnp.concatenate([k1, k0], axis=1), jnp.concatenate([k2, k1], axis=1)], axis=0
            )
            mf[a * W : (a + 1) * W, b * W : (b + 1) * W] = m
            mb[(2 - b) * W : (3 - b) * W, (2 - a) * W : (3 - a) * W] = m
    bias = jnp.concatenate([offs[...], offs[...]], axis=1)
    acc[...] = jnp.zeros_like(acc)
    bacc[...] = jnp.zeros_like(bacc)

    mark("transpose")
    @pl.loop(2, SX + 2)
    def _(r):
        ft[r] = fx[r, PAD : PAD + SY].T

    arrivals = [
        (top, fx.at[0:2, rows_y], 0), (bottom, fx.at[SX + 2 : SX + 4, rows_y], 1),
        (top, ux.at[0:1, rows_y], 2), (bottom, ux.at[SX + 1 : SX + 2, rows_y], 3),
        (left, rbuf.at[0, 0:48], 4), (right, rbuf.at[1, 0:48], 5),
        (jnp.logical_and(left, top), rbuf.at[0, 48:64], 6),
        (jnp.logical_and(left, bottom), rbuf.at[0, 64:80], 7),
        (jnp.logical_and(right, top), rbuf.at[1, 48:64], 8),
        (jnp.logical_and(right, bottom), rbuf.at[1, 64:80], 9),
    ]
    mark("await_rims")
    for there, dst, s in arrivals:
        @pl.when(there)
        def _(dst=dst, s=s):
            remote(dst, dst, hsem, s, s, at(0, 1)).wait_recv()

    mark("place_rims")
    ft[1] = fx[1, PAD : PAD + SY].T
    ft[SX + 2] = fx[SX + 2, PAD : PAD + SY].T

    for side in range(2):
        got = rbuf[side].astype(F32)
        rcol[side, 0, 2 : SX + 2] = got[0:16]
        rcol[side, 1, 2 : SX + 2] = got[16:32]
        for k in range(2):
            for n, row in ((k, 48), (SX + 2 + k, 64)):
                rcol[side, 0, n : n + 1] = got[row + k : row + k + 1]
                rcol[side, 1, n : n + 1] = got[row + 2 + k : row + 3 + k]
        ucol[side, 1 : SX + 1] = got[32:48]
        ucol[side, 0:1] = got[52:53]
        ucol[side, SX + 1 : SX + 2] = got[68:69]
        base = 0 if side == 0 else PAD + SY
        sub = lax.broadcasted_iota(jnp.int32, (8, W), 0)
        near, second = (7, 6) if side == 0 else (0, 1)
        empty = jnp.zeros((8, W), F32)

        def spread(rows):
            return jnp.broadcast_to(rows, (8, W))

        def padded(half):
            return jnp.concatenate([empty, half] if side == 0 else [half, empty], axis=0).astype(BF16)

        for r in range(SX + 4):
            other = jnp.where(sub == second, spread(rcol[side, 1, r : r + 1]), 0.0)
            half = jnp.where(sub == near, spread(rcol[side, 0, r : r + 1]), other)
            fx[r, base : base + PAD] = padded(half)
        for r in range(SX + 2):
            half = jnp.where(sub == near, spread(ucol[side, r : r + 1]), 0.0)
            ux[r, base : base + PAD] = padded(half)

    mark("forward")
    spot = lax.broadcasted_iota(jnp.int32, (SY, W), 0)

    def forward_row(r):
        window = jnp.concatenate([fx[r], fx[r + 1], fx[r + 2]], axis=1)
        p = jnp.dot(window, mf[...], preferred_element_type=F32)
        pre = (
            pltpu.roll(p[:, :W], 1, 0) + p[:, W : 2 * W] + pltpu.roll(p[:, 2 * W :], PY - 1, 0) + bias
        )
        sigma = jax.nn.sigmoid(pre)
        grad = (ux[r].astype(F32) * sigma * (1.0 + pre * (1.0 - sigma))).astype(BF16)
        gx_ref[r] = grad
        return pre, sigma, grad

    def weight_row(r):
        pre, sigma, grad = forward_row(r)
        act[r - 1] = (pre * sigma)[PAD : PAD + SY].astype(BF16)
        g32 = grad.astype(F32)
        inner = g32[PAD : PAD + SY]
        bacc[...] += inner.reshape(SY // 8, 8, W).sum(axis=0)
        gedge[0, pl.ds(r - 1, 1)] = inner[0:1]
        gedge[1, pl.ds(r - 1, 1)] = inner[SY - 1 : SY]
        after = pltpu.roll(g32, PY - 1, 0)[PAD : PAD + SY]
        before = pltpu.roll(g32, 1, 0)[PAD : PAD + SY]
        after = jnp.where(spot == SY - 1, 0.0, after).astype(BF16)
        before = jnp.where(spot == 0, 0.0, before).astype(BF16)
        return jnp.concatenate([after, grad[PAD : PAD + SY], before], axis=1)

    @pl.loop(0, SX // 16)
    def _(step):
        for k in range(0, 16, 4):
            r = step * 16 + k + 1
            rhs = jnp.concatenate([weight_row(r + n) for n in range(4)], axis=0)
            lhs = jnp.concatenate(
                [jnp.concatenate([ft[r + n + a] for n in range(4)], axis=1) for a in range(3)], axis=0
            )
            acc[...] += jnp.dot(lhs, rhs, preferred_element_type=F32)


    mark("rim_columns")

    for side in range(2):
        lhs = jnp.concatenate([rcol[side, 0, a + 1 : a + 1 + SX] for a in range(3)], axis=1)
        part = lax.dot_general(
            lhs.astype(BF16), gedge[side].astype(BF16), (((0,), (0,)), ((), ())), preferred_element_type=F32
        )
        acc[:, 2 * side * W : (2 * side + 1) * W] += part

    mark("pack")
    lane = lax.broadcasted_iota(jnp.int32, (CH, W), 1)

    def put(j, block):
        m = j // 2
        v[m // NX, m % NX, j % 2] = block

    highs = []
    for a in range(3):
        for b in range(3):
            t = acc[a * W : (a + 1) * W, b * W : (b + 1) * W]
            turned = pltpu.roll(t[CH:], CH, 1)
            put(3 * a + b, t[:CH] + jnp.where(lane < CH, turned, 0.0))
            highs.append((t[CH:], turned))
    total = jnp.sum(bacc[...], axis=0, keepdims=True)
    total = jnp.broadcast_to(total, (CH, W))
    highs.append((None, total + pltpu.roll(total, CH, 1)))
    for k in range(5):
        put(9 + k, jnp.where(lane < CH, highs[2 * k][0], highs[2 * k + 1][1]))
    for j in (14, 15):
        put(j, jnp.zeros((CH, W), F32))

    def input_rows(first, last):
        @pl.loop(first, last)
        def _(r):
            window = jnp.concatenate([gx_ref[r], gx_ref[r + 1], gx_ref[r + 2]], axis=1)
            p = lax.dot_general(
                window, mb[...], (((1,), (1,)), ((), ())), preferred_element_type=F32
            )
            out = pltpu.roll(p[:, :W], 1, 0) + p[:, W : 2 * W] + pltpu.roll(p[:, 2 * W :], PY - 1, 0)
            ig[r] = out[PAD : PAD + SY].astype(BF16)

    sent = []
    mark("sum_cores")
    first = remote(v.at[1 - c], cbuf, csem, 0, 0, device(x, z, h, 1 - c, d))
    first.start()
    sent.append(first)
    first.wait_recv()
    acc1[...] = v[c] + cbuf[...]
    acc1b[...] = acc1[...].astype(BF16)

    mark("sum_x")
    along = []
    for k in range(1, NX):
        other = (x + k) % NX
        copy = remote(acc1b.at[other], xbuf.at[k - 1], xsem, k - 1, k - 1, device(other, z, h, c, d))
        copy.start()
        along.append(copy)
    sent += along
    forward_row(0)
    forward_row(SX + 1)
    input_rows(0, 5)
    for copy in along:
        copy.wait_recv()
    pair = (acc1[x] + xbuf[0].astype(F32) + xbuf[1].astype(F32) + xbuf[2].astype(F32)).reshape(W, W).T
    for dd in range(ND):
        acc2[dd, 0] = pair[16 * dd : 16 * dd + 16].astype(BF16)
        acc2[dd, 1] = pair[CH + 16 * dd : CH + 16 * dd + 16].astype(BF16)

    mark("sum_y")
    ybuf[y] = acc2[d]
    for k in range(1, NYL):
        other = (y + k) % NYL
        copy = remote(
            acc2.at[other % ND], ybuf.at[y], ysem, k - 1, k - 1, device(x, z, other // ND, c, other % ND)
        )
        copy.start()
        sent.append(copy)
    input_rows(5, 11)
    for k in range(1, NYL):
        other = (y + NYL - k) % NYL
        slot = ybuf.at[other]
        remote(slot, slot, ysem, k - 1, k - 1, device(x, z, other // ND, c, other % ND)).wait_recv()
    part = ybuf[0].astype(F32)
    for k in range(1, NYL):
        part = part + ybuf[k].astype(F32)
    zbuf[z] = part.astype(BF16)

    mark("sum_z")
    for k in range(1, NZ):
        copy = remote(zbuf.at[z], zbuf.at[z], zsem, k - 1, k - 1, device(x, (z + k) % NZ, h, c, d))
        copy.start()
        sent.append(copy)
    input_rows(11, SX)
    for k in range(1, NZ):
        other = (z + NZ - k) % NZ
        slot = zbuf.at[other]
        remote(slot, slot, zsem, k - 1, k - 1, device(x, other, h, c, d)).wait_recv()
    part = zbuf[0].astype(F32)
    for k in range(1, NZ):
        part = part + zbuf[k].astype(F32)
    whole = part.astype(BF16)
    rest = (part - whole.astype(F32)).astype(BF16)
    lanes = lax.broadcasted_iota(jnp.int32, (2, 16, W), 2)
    halves = lax.broadcasted_iota(jnp.int32, (2, 16, W), 0)
    low_bias = jnp.logical_and(jnp.logical_and(lanes >= CH + 32, halves == 1), 4 * c + x == 6)
    gat[c, x] = jnp.where(low_bias, rest.astype(F32), whole.astype(F32)).astype(BF16)

    mark("gather")
    for j in range(1, NC * NX):
        copy = remote(gat.at[c, x], gat.at[c, x], gsem, j - 1, j - 1, gather_peer(x, z, h, c, d, j))
        copy.start()
        sent.append(copy)
    for j in range(1, NC * NX):
        px, pc = (x + NX - j // NC) % NX, (c + NC - j % NC) % NC
        slot = gat.at[pc, px]
        remote(slot, slot, gsem, j - 1, j - 1, device(px, z, h, pc, d)).wait_recv()

    mark("drain")
    for copy in sent:
        copy.wait_send()
    for there, dx, dy, src, dst, s, r in halos:
        @pl.when(there)
        def _(dx=dx, dy=dy, src=src, dst=dst, s=s, r=r):
            remote(src, dst, hsem, s, r, at(dx, dy)).wait_send()
    scopes.close()


def finish(scale, act_in, ig_in, gat, exps, act_hbm, ig_hbm, kg_ref, bg_ref, lsem):
    copies = [
        pltpu.make_async_copy(act_in, act_hbm, lsem.at[0]),
        pltpu.make_async_copy(ig_in, ig_hbm, lsem.at[1]),
    ]
    for copy in copies:
        copy.start()

    def tile(j, half):
        m = j // 2
        block = gat[m // NX, m % NX, half].astype(F32)
        return block if j % 2 == 0 else pltpu.roll(block, CH, 1)

    def scaled(value, a, b, k):
        factor = jnp.exp2(jnp.full((16, CH), exps[a, b, k], jnp.int32).astype(F32)) * scale
        kg_ref[a, b, k] = (value * factor).astype(BF16)

    for j in range(9):
        scaled(tile(j, 1)[:, :CH], j // 3, j % 3, 0)
        scaled(tile(j, 0)[:, :CH], j // 3, j % 3, 1)
        scaled(tile(9 + j // 2, j % 2)[:, :CH], j // 3, j % 3, 2)
    last = tile(13, 1)
    column = last[:, :16] + pltpu.roll(last, W - 32, 1)[:, :16]
    same = lax.broadcasted_iota(jnp.int32, (16, 16), 0) == lax.broadcasted_iota(jnp.int32, (16, 16), 1)
    bg_ref[...] = jnp.sum(jnp.where(same, column, 0.0), axis=0, keepdims=True) * scale
    for copy in copies:
        copy.wait()


def local(features, kernel, offsets, upstream, grad_exponents):
    count = 4 * GX * GY * SX * SY * 2
    vmem, anywhere = pltpu.VMEM, pl.BlockSpec(memory_space=pl.ANY)
    hbm = pl.BlockSpec(memory_space=pltpu.HBM)
    in_vmem = pl.BlockSpec(memory_space=pltpu.VMEM)
    dma = pltpu.SemaphoreType.DMA
    activation, input_grad, gathered = pl.pallas_call(
        body,
        out_shape=(
            jax.ShapeDtypeStruct((SX, SY, W), BF16),
            jax.ShapeDtypeStruct((SX, SY, W), BF16),
            jax.ShapeDtypeStruct((NC, NX, 2, 16, W), BF16),
        ),
        in_specs=[hbm, hbm, hbm, hbm],
        out_specs=(in_vmem, in_vmem, in_vmem),
        scratch_shapes=[
            vmem((SX + 4, PY, W), BF16),
            vmem((SX + 2, PY, W), BF16),
            vmem((SX + 2, PY, W), BF16),
            vmem((SX + 4, W, SY), BF16),
            vmem((3 * W, 3 * W), BF16),
            vmem((3 * W, 3 * W), BF16),
            vmem((3 * W, 3 * W), F32),
            vmem((8, W), F32),
            vmem((2, PACK, W), F32),
            vmem((2, PACK, W), BF16),
            vmem((2, PACK, W), BF16),
            vmem((2, 2, 24, W), F32),
            vmem((2, 24, W), F32),
            vmem((2, SX, W), F32),
            vmem((NC, NX, 2, CH, W), F32),
            vmem((NX, 2, CH, W), F32),
            vmem((NX, 2, CH, W), F32),
            vmem((NX, 2, CH, W), BF16),
            vmem((NX - 1, 2, CH, W), BF16),
            vmem((ND, 2, 16, W), BF16),
            vmem((NYL, 2, 16, W), BF16),
            vmem((NZ, 2, 16, W), BF16),
            vmem((3, 3, 3, CH, CH), BF16),
            vmem((1, CH), F32),
            dma((4,)),
            dma((2, 10)),
            dma((2, 1)),
            dma((2, NX - 1)),
            dma((2, NYL - 1)),
            dma((2, NZ - 1)),
            dma((2, NC * NX - 1)),
        ],
        compiler_params=pltpu.CompilerParams(
            collective_id=0, has_side_effects=True, vmem_limit_bytes=24 << 20
        ),
    )(
        pltpu.with_memory_space_constraint(features.reshape(SX, SY, W), pltpu.HBM),
        pltpu.with_memory_space_constraint(upstream.reshape(SX, SY, W), pltpu.HBM),
        pltpu.with_memory_space_constraint(kernel, pltpu.HBM),
        pltpu.with_memory_space_constraint(offsets.reshape(1, CH), pltpu.HBM),
    )
    activation, input_grad, kernel_grad, bias_grad = pl.pallas_call(
        functools.partial(finish, 1.0 / math.sqrt(count)),
        out_shape=(
            jax.ShapeDtypeStruct((SX, SY, W), BF16),
            jax.ShapeDtypeStruct((SX, SY, W), BF16),
            jax.ShapeDtypeStruct((3, 3, 3, 16, CH), BF16),
            jax.ShapeDtypeStruct((1, 16), F32),
        ),
        in_specs=[in_vmem, in_vmem, in_vmem, pl.BlockSpec(memory_space=pltpu.SMEM)],
        out_specs=(hbm, hbm, in_vmem, in_vmem),
        scratch_shapes=[dma((2,))],
        compiler_params=pltpu.CompilerParams(vmem_limit_bytes=24 << 20),
    )(activation, input_grad, gathered, grad_exponents)
    kernel_grad = kernel_grad.swapaxes(3, 4)
    return (
        activation.reshape(features.shape),
        input_grad.reshape(features.shape),
        kernel_grad,
        bias_grad.reshape(16),
    )


def solution(mesh):
    placed = (P("dp", "gx", "gy", None), P(), P(), P("dp", "gx", "gy", None), P())
    return jax.shard_map(
        local,
        mesh=mesh,
        in_specs=placed,
        out_specs=(
            P("dp", "gx", "gy", None),
            P("dp", "gx", "gy", None),
            P(None, None, None, None, "dp"),
            P("dp"),
        ),
        check_vma=False,
    )
```

```python
import contextlib
import functools
import math

import jax
import jax.numpy as jnp
from jax import lax
from jax.experimental import pallas as pl
from jax.experimental.pallas import tpu as pltpu
from jax.sharding import PartitionSpec as P

MESH = pl.DeviceIdType.MESH
F32, BF16 = jnp.float32, jnp.bfloat16

NX, NZ, NH, NC, ND = 4, 8, 2, 2, 4
NYL = NH * ND
GX, GY = NX * NZ, NH * NC

SX, SY, W, CH, PAD = 16, 256, 128, 64, 16
PY = SY + 2 * PAD
PACK = 80

FAR_FIRST = (4, 3, 5, 2, 6, 1, 7)


def place():
    gx, gy, d = lax.axis_index("gx"), lax.axis_index("gy"), lax.axis_index("dp")
    return gx // NZ, gx % NZ, gy // NC, gy % NC, d


def device(x, z, h, c, d):
    return {"gx": x * NZ + z, "gy": h * NC + c, "dp": d}


def gather_peer(x, z, h, c, d, j):
    return device((x + j // NC) % NX, z, h, (c + j) % NC, d)


def body(
    f_hbm, u_hbm, k_hbm, o_hbm, act, ig, gat,
    fx, ux, gx_ref, ft, mf, mb, acc, bacc, e32, ebf, rbuf, rcol, ucol, gedge,
    v, cbuf, acc1, acc1b, xbuf, acc2, ybuf, zbuf, kern, offs,
    lsem, hsem, csem, xsem, ysem, zsem, gsem,
):
    scopes = contextlib.ExitStack()

    def mark(name):
        scopes.close()
        scopes.enter_context(jax.named_scope(name))

    x, z, h, c, d = place()
    gx, gy = lax.axis_index("gx"), lax.axis_index("gy")
    y = h * ND + d

    def at(dx, dy):
        return {"gx": (gx + dx + GX) % GX, "gy": (gy + dy + GY) % GY, "dp": d}

    def remote(src, dst, sems, s, r, peer):
        return pltpu.make_async_remote_copy(
            src_ref=src, dst_ref=dst, send_sem=sems.at[0, s], recv_sem=sems.at[1, r],
            device_id=peer, device_id_type=MESH,
        )

    mark("setup")
    load_f = pltpu.make_async_copy(f_hbm, fx.at[2 : 2 + SX, PAD : PAD + SY], lsem.at[0])
    load_u = pltpu.make_async_copy(u_hbm, ux.at[1 : 1 + SX, PAD : PAD + SY], lsem.at[1])
    load_k = pltpu.make_async_copy(k_hbm, kern, lsem.at[2])
    load_o = pltpu.make_async_copy(o_hbm, offs, lsem.at[3])
    load_k.start()
    load_o.start()
    load_f.start()
    load_u.start()

    top, bottom, left, right = gx > 0, gx < GX - 1, gy > 0, gy < GY - 1

    barrier = pltpu.get_barrier_semaphore()
    around = [at(dx, dy) for dx in (-1, 0, 1) for dy in (-1, 0, 1) if dx or dy]
    others = [gather_peer(x, z, h, c, d, j) for j in range(1, NC * NX)]
    for k in range(1, NYL):
        other = (y + k) % NYL
        others.append(device(x, z, other // ND, c, other % ND))
    for k in range(1, NZ):
        others.append(device(x, (z + k) % NZ, h, c, d))
    for peer in around + others:
        pl.semaphore_signal(barrier, inc=1, device_id=peer, device_id_type=MESH)

    mark("barrier")
    pl.semaphore_wait(barrier, len(around) + len(others))

    mark("send_rims")
    rows_y = slice(PAD, PAD + SY)
    halos = [
        (top, -1, 0, f_hbm.at[0:2], fx.at[SX + 2 : SX + 4, rows_y], 0, 1),
        (top, -1, 0, u_hbm.at[0:1], ux.at[SX + 1 : SX + 2, rows_y], 2, 3),
        (bottom, 1, 0, f_hbm.at[SX - 2 : SX], fx.at[0:2, rows_y], 1, 0),
        (bottom, 1, 0, u_hbm.at[SX - 1 : SX], ux.at[0:1, rows_y], 3, 2),
        (left, 0, -1, ebf.at[0, 0:48], rbuf.at[1, 0:48], 4, 5),
        (right, 0, 1, ebf.at[1, 0:48], rbuf.at[0, 0:48], 5, 4),
        (jnp.logical_and(left, top), -1, -1, ebf.at[0, 48:64], rbuf.at[1, 64:80], 6, 9),
        (jnp.logical_and(left, bottom), 1, -1, ebf.at[0, 64:80], rbuf.at[1, 48:64], 7, 8),
        (jnp.logical_and(right, top), -1, 1, ebf.at[1, 48:64], rbuf.at[0, 64:80], 8, 7),
        (jnp.logical_and(right, bottom), 1, 1, ebf.at[1, 64:80], rbuf.at[0, 48:64], 9, 6),
    ]
    for there, dx, dy, src, dst, s, r in halos[:4]:
        @pl.when(there)
        def _(dx=dx, dy=dy, src=src, dst=dst, s=s, r=r):
            remote(src, dst, hsem, s, r, at(dx, dy)).start()

    mark("rims")
    load_f.wait()
    load_u.wait()
    e32[...] = jnp.zeros_like(e32)

    for r in range(SX):
        for side, base in ((0, PAD), (1, PAD + SY - 16)):
            near, second = (0, 1) if side == 0 else (15, 14)
            tf = fx[2 + r, base : base + 16].astype(F32)
            tu = ux[1 + r, base : base + 16].astype(F32)
            nf, sf, nu = tf[near : near + 1], tf[second : second + 1], tu[near : near + 1]
            e32[side, r : r + 1] = nf
            e32[side, 16 + r : 17 + r] = sf
            e32[side, 32 + r : 33 + r] = nu
            for corner, first, edge in ((48, 0, 0), (64, SX - 2, SX - 1)):
                if first <= r < first + 2:
                    k = corner + r - first
                    e32[side, k : k + 1] = nf
                    e32[side, k + 2 : k + 3] = sf
                if r == edge:
                    e32[side, corner + 4 : corner + 5] = nu
    ebf[...] = e32[...].astype(BF16)

    for there, dx, dy, src, dst, s, r in halos[6:] + halos[4:6]:
        @pl.when(there)
        def _(dx=dx, dy=dy, src=src, dst=dst, s=s, r=r):
            remote(src, dst, hsem, s, r, at(dx, dy)).start()

    mark("matrices")
    def blank(ref, *where):
        ref[where] = jnp.zeros(ref[where].shape, ref.dtype)

    @pl.when(jnp.logical_not(top))
    def _():
        blank(fx, slice(0, 2), slice(PAD, PAD + SY))
        blank(ux, slice(0, 1), slice(PAD, PAD + SY))

    @pl.when(jnp.logical_not(bottom))
    def _():
        blank(fx, slice(SX + 2, SX + 4), slice(PAD, PAD + SY))
        blank(ux, slice(SX + 1, SX + 2), slice(PAD, PAD + SY))

    for side, there in ((0, left), (1, right)):
        for rows, other in ((slice(0, 48), True), (slice(48, 64), top), (slice(64, 80), bottom)):
            @pl.when(jnp.logical_not(jnp.logical_and(there, other)))
            def _(side=side, rows=rows):
                blank(rbuf, side, rows)

    load_k.wait()
    load_o.wait()
    for a in range(3):
        for b in range(3):
            k0, k1, k2 = kern[a, b, 0], kern[a, b, 1], kern[a, b, 2]
            m = jnp.concatenate(
                [jnp.concatenate([k1, k0], axis=1), jnp.concatenate([k2, k1], axis=1)], axis=0
            )
            mf[a * W : (a + 1) * W, b * W : (b + 1) * W] = m
            mb[(2 - b) * W : (3 - b) * W, (2 - a) * W : (3 - a) * W] = m
    bias = jnp.concatenate([offs[...], offs[...]], axis=1)
    acc[...] = jnp.zeros_like(acc)
    bacc[...] = jnp.zeros_like(bacc)

    mark("transpose")
    @pl.loop(2, SX + 2)
    def _(r):
        ft[r] = fx[r, PAD : PAD + SY].T

    arrivals = [
        (top, fx.at[0:2, rows_y], 0), (bottom, fx.at[SX + 2 : SX + 4, rows_y], 1),
        (top, ux.at[0:1, rows_y], 2), (bottom, ux.at[SX + 1 : SX + 2, rows_y], 3),
        (left, rbuf.at[0, 0:48], 4), (right, rbuf.at[1, 0:48], 5),
        (jnp.logical_and(left, top), rbuf.at[0, 48:64], 6),
        (jnp.logical_and(left, bottom), rbuf.at[0, 64:80], 7),
        (jnp.logical_and(right, top), rbuf.at[1, 48:64], 8),
        (jnp.logical_and(right, bottom), rbuf.at[1, 64:80], 9),
    ]
    mark("await_rims")
    for there, dst, s in arrivals:
        @pl.when(there)
        def _(dst=dst, s=s):
            remote(dst, dst, hsem, s, s, at(0, 1)).wait_recv()

    mark("place_rims")
    ft[1] = fx[1, PAD : PAD + SY].T
    ft[SX + 2] = fx[SX + 2, PAD : PAD + SY].T

    for side in range(2):
        got = rbuf[side].astype(F32)
        rcol[side, 0, 2 : SX + 2] = got[0:16]
        rcol[side, 1, 2 : SX + 2] = got[16:32]
        for k in range(2):
            for n, row in ((k, 48), (SX + 2 + k, 64)):
                rcol[side, 0, n : n + 1] = got[row + k : row + k + 1]
                rcol[side, 1, n : n + 1] = got[row + 2 + k : row + 3 + k]
        ucol[side, 1 : SX + 1] = got[32:48]
        ucol[side, 0:1] = got[52:53]
        ucol[side, SX + 1 : SX + 2] = got[68:69]
        base = 0 if side == 0 else PAD + SY
        sub = lax.broadcasted_iota(jnp.int32, (8, W), 0)
        near, second = (7, 6) if side == 0 else (0, 1)
        empty = jnp.zeros((8, W), F32)

        def spread(rows):
            return jnp.broadcast_to(rows, (8, W))

        def padded(half):
            return jnp.concatenate([empty, half] if side == 0 else [half, empty], axis=0).astype(BF16)

        for r in range(SX + 4):
            other = jnp.where(sub == second, spread(rcol[side, 1, r : r + 1]), 0.0)
            half = jnp.where(sub == near, spread(rcol[side, 0, r : r + 1]), other)
            fx[r, base : base + PAD] = padded(half)
        for r in range(SX + 2):
            half = jnp.where(sub == near, spread(ucol[side, r : r + 1]), 0.0)
            ux[r, base : base + PAD] = padded(half)

    mark("forward")
    spot = lax.broadcasted_iota(jnp.int32, (SY, W), 0)

    def forward_row(r):
        window = jnp.concatenate([fx[r], fx[r + 1], fx[r + 2]], axis=1)
        p = jnp.dot(window, mf[...], preferred_element_type=F32)
        pre = (
            pltpu.roll(p[:, :W], 1, 0) + p[:, W : 2 * W] + pltpu.roll(p[:, 2 * W :], PY - 1, 0) + bias
        )
        sigma = jax.nn.sigmoid(pre)
        grad = (ux[r].astype(F32) * sigma * (1.0 + pre * (1.0 - sigma))).astype(BF16)
        gx_ref[r] = grad
        return pre, sigma, grad

    def weight_row(r):
        pre, sigma, grad = forward_row(r)
        act[r - 1] = (pre * sigma)[PAD : PAD + SY].astype(BF16)
        g32 = grad.astype(F32)
        inner = g32[PAD : PAD + SY]
        bacc[...] += inner.reshape(SY // 8, 8, W).sum(axis=0)
        gedge[0, pl.ds(r - 1, 1)] = inner[0:1]
        gedge[1, pl.ds(r - 1, 1)] = inner[SY - 1 : SY]
        after = pltpu.roll(g32, PY - 1, 0)[PAD : PAD + SY]
        before = pltpu.roll(g32, 1, 0)[PAD : PAD + SY]
        after = jnp.where(spot == SY - 1, 0.0, after).astype(BF16)
        before = jnp.where(spot == 0, 0.0, before).astype(BF16)
        return jnp.concatenate([after, grad[PAD : PAD + SY], before], axis=1)

    @pl.loop(0, SX // 16)
    def _(step):
        for k in range(0, 16, 4):
            r = step * 16 + k + 1
            rhs = jnp.concatenate([weight_row(r + n) for n in range(4)], axis=0)
            lhs = jnp.concatenate(
                [jnp.concatenate([ft[r + n + a] for n in range(4)], axis=1) for a in range(3)], axis=0
            )
            acc[...] += jnp.dot(lhs, rhs, preferred_element_type=F32)


    mark("rim_columns")

    for side in range(2):
        lhs = jnp.concatenate([rcol[side, 0, a + 1 : a + 1 + SX] for a in range(3)], axis=1)
        part = lax.dot_general(
            lhs.astype(BF16), gedge[side].astype(BF16), (((0,), (0,)), ((), ())), preferred_element_type=F32
        )
        acc[:, 2 * side * W : (2 * side + 1) * W] += part

    mark("pack")
    lane = lax.broadcasted_iota(jnp.int32, (CH, W), 1)

    def put(j, block):
        m = j // 2
        v[m // NX, m % NX, j % 2] = block

    highs = []
    for a in range(3):
        for b in range(3):
            t = acc[a * W : (a + 1) * W, b * W : (b + 1) * W]
            turned = pltpu.roll(t[CH:], CH, 1)
            put(3 * a + b, t[:CH] + jnp.where(lane < CH, turned, 0.0))
            highs.append((t[CH:], turned))
    total = jnp.sum(bacc[...], axis=0, keepdims=True)
    total = jnp.broadcast_to(total, (CH, W))
    highs.append((None, total + pltpu.roll(total, CH, 1)))
    for k in range(5):
        put(9 + k, jnp.where(lane < CH, highs[2 * k][0], highs[2 * k + 1][1]))
    for j in (14, 15):
        put(j, jnp.zeros((CH, W), F32))

    def input_rows(first, last):
        @pl.loop(first, last)
        def _(r):
            window = jnp.concatenate([gx_ref[r], gx_ref[r + 1], gx_ref[r + 2]], axis=1)
            p = lax.dot_general(
                window, mb[...], (((1,), (1,)), ((), ())), preferred_element_type=F32
            )
            out = pltpu.roll(p[:, :W], 1, 0) + p[:, W : 2 * W] + pltpu.roll(p[:, 2 * W :], PY - 1, 0)
            ig[r] = out[PAD : PAD + SY].astype(BF16)

    sent = []
    mark("sum_cores")
    first = remote(v.at[1 - c], cbuf, csem, 0, 0, device(x, z, h, 1 - c, d))
    first.start()
    sent.append(first)
    first.wait_recv()
    acc1[...] = v[c] + cbuf[...]
    acc1b[...] = acc1[...].astype(BF16)

    mark("sum_x")
    along = []
    for k in (2, 1, 3):
        other = (x + k) % NX
        copy = remote(acc1b.at[other], xbuf.at[k - 1], xsem, k - 1, k - 1, device(other, z, h, c, d))
        copy.start()
        along.append(copy)
    sent += along
    forward_row(0)
    forward_row(SX + 1)
    input_rows(0, 5)
    for copy in along:
        copy.wait_recv()
    pair = (acc1[x] + xbuf[0].astype(F32) + xbuf[1].astype(F32) + xbuf[2].astype(F32)).reshape(W, W).T
    for dd in range(ND):
        acc2[dd, 0] = pair[16 * dd : 16 * dd + 16].astype(BF16)
        acc2[dd, 1] = pair[CH + 16 * dd : CH + 16 * dd + 16].astype(BF16)

    mark("sum_y")
    ybuf[y] = acc2[d]
    for k in FAR_FIRST:
        other = (y + k) % NYL
        copy = remote(
            acc2.at[other % ND], ybuf.at[y], ysem, k - 1, k - 1, device(x, z, other // ND, c, other % ND)
        )
        copy.start()
        sent.append(copy)
    input_rows(5, 11)
    for k in range(1, NYL):
        other = (y + NYL - k) % NYL
        slot = ybuf.at[other]
        remote(slot, slot, ysem, k - 1, k - 1, device(x, z, other // ND, c, other % ND)).wait_recv()
    part = ybuf[0].astype(F32)
    for k in range(1, NYL):
        part = part + ybuf[k].astype(F32)
    zbuf[z] = part.astype(BF16)

    mark("sum_z")
    for k in FAR_FIRST:
        copy = remote(zbuf.at[z], zbuf.at[z], zsem, k - 1, k - 1, device(x, (z + k) % NZ, h, c, d))
        copy.start()
        sent.append(copy)
    input_rows(11, SX)
    for k in range(1, NZ):
        other = (z + NZ - k) % NZ
        slot = zbuf.at[other]
        remote(slot, slot, zsem, k - 1, k - 1, device(x, other, h, c, d)).wait_recv()
    part = zbuf[0].astype(F32)
    for k in range(1, NZ):
        part = part + zbuf[k].astype(F32)
    whole = part.astype(BF16)
    rest = (part - whole.astype(F32)).astype(BF16)
    lanes = lax.broadcasted_iota(jnp.int32, (2, 16, W), 2)
    halves = lax.broadcasted_iota(jnp.int32, (2, 16, W), 0)
    low_bias = jnp.logical_and(jnp.logical_and(lanes >= CH + 32, halves == 1), 4 * c + x == 6)
    gat[c, x] = jnp.where(low_bias, rest.astype(F32), whole.astype(F32)).astype(BF16)

    mark("gather")
    for j in (4, 5, 2, 3, 6, 7, 1):
        copy = remote(gat.at[c, x], gat.at[c, x], gsem, j - 1, j - 1, gather_peer(x, z, h, c, d, j))
        copy.start()
        sent.append(copy)
    for j in range(1, NC * NX):
        px, pc = (x + NX - j // NC) % NX, (c + NC - j % NC) % NC
        slot = gat.at[pc, px]
        remote(slot, slot, gsem, j - 1, j - 1, device(px, z, h, pc, d)).wait_recv()

    mark("drain")
    for copy in sent:
        copy.wait_send()
    for there, dx, dy, src, dst, s, r in halos:
        @pl.when(there)
        def _(dx=dx, dy=dy, src=src, dst=dst, s=s, r=r):
            remote(src, dst, hsem, s, r, at(dx, dy)).wait_send()
    scopes.close()


def finish(scale, act_in, ig_in, gat, exps, act_hbm, ig_hbm, kg_ref, bg_ref, lsem):
    copies = [
        pltpu.make_async_copy(act_in, act_hbm, lsem.at[0]),
        pltpu.make_async_copy(ig_in, ig_hbm, lsem.at[1]),
    ]
    for copy in copies:
        copy.start()

    def tile(j, half):
        m = j // 2
        block = gat[m // NX, m % NX, half].astype(F32)
        return block if j % 2 == 0 else pltpu.roll(block, CH, 1)

    def scaled(value, a, b, k):
        factor = jnp.exp2(jnp.full((16, CH), exps[a, b, k], jnp.int32).astype(F32)) * scale
        kg_ref[a, b, k] = (value * factor).astype(BF16)

    for j in range(9):
        scaled(tile(j, 1)[:, :CH], j // 3, j % 3, 0)
        scaled(tile(j, 0)[:, :CH], j // 3, j % 3, 1)
        scaled(tile(9 + j // 2, j % 2)[:, :CH], j // 3, j % 3, 2)
    last = tile(13, 1)
    column = last[:, :16] + pltpu.roll(last, W - 32, 1)[:, :16]
    same = lax.broadcasted_iota(jnp.int32, (16, 16), 0) == lax.broadcasted_iota(jnp.int32, (16, 16), 1)
    bg_ref[...] = jnp.sum(jnp.where(same, column, 0.0), axis=0, keepdims=True) * scale
    for copy in copies:
        copy.wait()


def local(features, kernel, offsets, upstream, grad_exponents):
    count = 4 * GX * GY * SX * SY * 2
    vmem, anywhere = pltpu.VMEM, pl.BlockSpec(memory_space=pl.ANY)
    hbm = pl.BlockSpec(memory_space=pltpu.HBM)
    in_vmem = pl.BlockSpec(memory_space=pltpu.VMEM)
    dma = pltpu.SemaphoreType.DMA
    activation, input_grad, gathered = pl.pallas_call(
        body,
        out_shape=(
            jax.ShapeDtypeStruct((SX, SY, W), BF16),
            jax.ShapeDtypeStruct((SX, SY, W), BF16),
            jax.ShapeDtypeStruct((NC, NX, 2, 16, W), BF16),
        ),
        in_specs=[hbm, hbm, hbm, hbm],
        out_specs=(in_vmem, in_vmem, in_vmem),
        scratch_shapes=[
            vmem((SX + 4, PY, W), BF16),
            vmem((SX + 2, PY, W), BF16),
            vmem((SX + 2, PY, W), BF16),
            vmem((SX + 4, W, SY), BF16),
            vmem((3 * W, 3 * W), BF16),
            vmem((3 * W, 3 * W), BF16),
            vmem((3 * W, 3 * W), F32),
            vmem((8, W), F32),
            vmem((2, PACK, W), F32),
            vmem((2, PACK, W), BF16),
            vmem((2, PACK, W), BF16),
            vmem((2, 2, 24, W), F32),
            vmem((2, 24, W), F32),
            vmem((2, SX, W), F32),
            vmem((NC, NX, 2, CH, W), F32),
            vmem((NX, 2, CH, W), F32),
            vmem((NX, 2, CH, W), F32),
            vmem((NX, 2, CH, W), BF16),
            vmem((NX - 1, 2, CH, W), BF16),
            vmem((ND, 2, 16, W), BF16),
            vmem((NYL, 2, 16, W), BF16),
            vmem((NZ, 2, 16, W), BF16),
            vmem((3, 3, 3, CH, CH), BF16),
            vmem((1, CH), F32),
            dma((4,)),
            dma((2, 10)),
            dma((2, 1)),
            dma((2, NX - 1)),
            dma((2, NYL - 1)),
            dma((2, NZ - 1)),
            dma((2, NC * NX - 1)),
        ],
        compiler_params=pltpu.CompilerParams(
            collective_id=0, has_side_effects=True, vmem_limit_bytes=24 << 20
        ),
    )(
        pltpu.with_memory_space_constraint(features.reshape(SX, SY, W), pltpu.HBM),
        pltpu.with_memory_space_constraint(upstream.reshape(SX, SY, W), pltpu.HBM),
        pltpu.with_memory_space_constraint(kernel, pltpu.HBM),
        pltpu.with_memory_space_constraint(offsets.reshape(1, CH), pltpu.HBM),
    )
    activation, input_grad, kernel_grad, bias_grad = pl.pallas_call(
        functools.partial(finish, 1.0 / math.sqrt(count)),
        out_shape=(
            jax.ShapeDtypeStruct((SX, SY, W), BF16),
            jax.ShapeDtypeStruct((SX, SY, W), BF16),
            jax.ShapeDtypeStruct((3, 3, 3, 16, CH), BF16),
            jax.ShapeDtypeStruct((1, 16), F32),
        ),
        in_specs=[in_vmem, in_vmem, in_vmem, pl.BlockSpec(memory_space=pltpu.SMEM)],
        out_specs=(hbm, hbm, in_vmem, in_vmem),
        scratch_shapes=[dma((2,))],
        compiler_params=pltpu.CompilerParams(vmem_limit_bytes=24 << 20),
    )(activation, input_grad, gathered, grad_exponents)
    kernel_grad = kernel_grad.swapaxes(3, 4)
    return (
        activation.reshape(features.shape),
        input_grad.reshape(features.shape),
        kernel_grad,
        bias_grad.reshape(16),
    )


def solution(mesh):
    placed = (P("dp", "gx", "gy", None), P(), P(), P("dp", "gx", "gy", None), P())
    return jax.shard_map(
        local,
        mesh=mesh,
        in_specs=placed,
        out_specs=(
            P("dp", "gx", "gy", None),
            P("dp", "gx", "gy", None),
            P(None, None, None, None, "dp"),
            P("dp"),
        ),
        check_vma=False,
    )
```
